32 devices in a mesh: dp: 4 (over z), expert: 8 (over y, x, core).
Axes of the slice: x: 2, y: 2, z: 4, core: 2. Of those that a mesh axis runs over, the one named last changes fastest.
Arguments:
- tokens: bfloat16 [2, 8, 1024, 1024], P(None, 'expert', 'dp'), may hold values from -6 to 6
- cotangent: float32 [2, 8, 1024, 1024], P(None, 'expert', 'dp'), may hold values from -6 to 6
- routes: int32 [2, 8, 1024, 1], P(None, 'expert', 'dp'), may hold values from 0 to 7; in each aligned block of 256 rows (0 to 255, 256 to 511, ..., all dimensions but the last counted through in order) at most 40 rows name the same one
- prefix: int32 [2, 8], P(None, 'expert'), may hold values from 0 to 1024
- qkv_weight: bfloat16 [1024, 3072], P(('dp', 'expert')), may hold values from -0.25 to 0.25
- mix_weight: bfloat16 [1024, 1024], P(('dp', 'expert')), may hold values from -0.75 to 0.75
- up_weight: bfloat16 [1024, 4096], P(('dp', 'expert')), may hold values from -0.1875 to 0.1875
- down_weight: bfloat16 [4096, 1024], P(('dp', 'expert')), may hold values from -0.09375 to 0.09375
- dense_gain: bfloat16 [2, 1024], P(None, ('dp', 'expert')), may hold values from 0.5 to 1.5
- expert_up: bfloat16 [8, 2, 1024, 4096], P('expert', None, None, 'dp'), may hold values from -0.1875 to 0.1875
- expert_down: bfloat16 [8, 2, 4096, 1024], P('expert', None, 'dp'), may hold values from -0.09375 to 0.09375
- expert_gain: bfloat16 [8, 2, 1024], P('expert'), may hold values from 0.5 to 1.5
- centroids: bfloat16 [8, 1024], P('expert'), may hold values from -0.13085938 to 0.13085938
Outputs:
- outputs: bfloat16 [2, 8, 1024, 1024], P(None, 'expert', 'dp')
- input_grad: float32 [2, 8, 1024, 1024], P(None, 'expert', 'dp')
- qkv_grad: float32 [1024, 3072], P(('dp', 'expert'))
- mix_grad: float32 [1024, 1024], P(('dp', 'expert'))
- up_grad: float32 [1024, 4096], P(('dp', 'expert'))
- down_grad: float32 [4096, 1024], P(('dp', 'expert'))
- dense_gain_grad: float32 [2, 1024], P(None, ('dp', 'expert'))
- expert_up_grad: float32 [8, 2, 1024, 4096], P('expert', None, None, 'dp')
- expert_down_grad: float32 [8, 2, 4096, 1024], P('expert', None, 'dp')
- expert_gain_grad: float32 [8, 2, 1024], P('expert')
- centroid_grad: float32 [8, 1024], P('expert')
- branch_rms: float32 [4, 2, 8], P(None, None, 'expert')
The draws below stay inside these ranges and needn't reach their ends.
Inputs may be any that keep to these rules, and one draw needn't show every extreme that they name: `routes`: in each aligned block of 256 rows (one sequence's tokens on one index of dp) no expert is named by more than 40 rows, a bound that some block reaches.
All inputs are finite; a program needn't handle non-finite values.
Results may differ from the reference program's by a relative error of at most 0.018.
Values may be sent and summed in bfloat16 or wider, within the bound.
No kernel may reach another device: no remote copies, remote signals or barrier semaphores. Data moves between devices by JAX's collectives and lax.ppermute only.
A program may use at most 384 MiB of HBM per device.

```python
import math
import jax
import jax.numpy as jnp
import numpy as np
from jax import lax

D = 1024
HEAD_DIM = 64
FF = 4096
EFF = 4096
TOK_MB = 256
MICRO = 2
SEQS = 8
EXPERTS = 8
LENGTH = 1024
CAP = 40


def with_ends(result, rng, low, high):
    longest = result.shape.index(max(result.shape))
    spots = []
    for shift in (0, 1):
        where = [jax.random.randint(jax.random.fold_in(rng, axis), (), 0, length) for axis, length in enumerate(result.shape)]
        where[longest] = (where[longest] + shift) % result.shape[longest]
        spots.append(tuple(where))
    return result.at[spots[0]].set(low).at[spots[1]].set(high)


def levels(key, dims, shards, least, largest):
    factor_of, own = 1.0, jax.random.fold_in(key, 6)
    for dim, shards_of in shards:
        heights = jnp.exp(jax.random.uniform(jax.random.fold_in(own, dim), (shards_of,), jnp.float32, least / len(shards), largest / len(shards)))
        factor_of = factor_of * jnp.repeat(heights, dims[dim] // shards_of).reshape([-1 if axis == dim else 1 for axis in range(len(dims))])
    return factor_of


def routed_block(rng, own, number, rows, number_of, top, bound, lean):
    ranking = jax.random.permutation(rng, number_of)
    packed, usual = shares(number_of, rows * top, bound, lean, True), shares(number_of, rows * top, bound, lean, False)
    places = jnp.arange(number_of)

    def named(tallies, rotation):
        used = int((tallies > 0).sum())
        fixed = max(1, used // 4)
        passed = fixed + (places - fixed + rotation * (used - fixed)) % max(1, number_of - fixed)
        return jnp.zeros((number_of,), jnp.int32).at[ranking[jnp.where(places < fixed, places, passed)]].set(jnp.asarray(tallies, jnp.int32))

    tallies = jnp.where(number % 4 == 0, named(packed, number // 4), named(usual, number - number // 4 - 1))
    mixed = jax.random.permutation(jax.random.fold_in(own, 3), number_of)
    donor, receiver = mixed[0:number_of // 2 * 2:2], mixed[1:number_of // 2 * 2:2]
    room = jnp.minimum(tallies[donor] - 1, bound - tallies[receiver]) // 2
    room = jnp.where((donor == ranking[0]) | (receiver == ranking[0]) | (tallies[receiver] == 0), 0, jnp.maximum(room, 0))
    passed = jax.random.randint(jax.random.fold_in(own, 4), (number_of // 2,), 0, 1 << 20) % (room + 1)
    tallies = tallies.at[donor].add(-passed).at[receiver].add(passed)
    members = jnp.searchsorted(jnp.cumsum(tallies), jnp.arange(rows * top), side="right").astype(jnp.int32)
    listing = members.reshape(top, rows).T
    listing = listing[jax.random.permutation(jax.random.fold_in(own, 1), rows)]
    rotation = jax.random.randint(jax.random.fold_in(own, 2), (rows, 1), 0, top)
    return jnp.take_along_axis(listing, (jnp.arange(top)[None, :] + rotation) % top, axis=1)


def shares(count, total, bound, slope, full):
    loads = [(1 << 20) // math.isqrt(standing ** slope) + 1 for standing in range(1, count + 1)]
    largest = bound if full else min(bound, max(-(-total // count), total * loads[0] // sum(loads)))
    least = 1 if total - largest >= count - 1 else 0
    counts, rest = [largest] + [least] * (count - 1), total - largest - least * (count - 1)
    while rest > 0:
        candidates = [i for i in range(1, count) if counts[i] < largest] or [i for i in range(1, count) if counts[i] < bound]
        whole, left = sum([loads[i] for i in candidates]), rest
        for i in candidates:
            addition = min(bound - counts[i], max(1, left * loads[i] // whole), rest)
            counts[i] = counts[i] + addition
            rest = rest - addition
    return np.array(counts)


def bell_draw(stream_key, extent, deviation, bound, split=(), held_as=jnp.bfloat16):
    result = jax.random.normal(stream_key, extent, jnp.float32) * deviation
    if len(split) > 0:
        result = levels(stream_key, extent, split, -0.22, 0.18) * result
    return jnp.clip(result, min=-bound, max=bound).astype(held_as)


def setup_inputs(seed: int = 0) -> dict:
    key_of = jax.random.split(jax.random.key(seed), 14)
    tokens = bell_draw(key_of[0], (MICRO, SEQS, LENGTH, D), 1.0, 6.0, ((1, 8), (2, 4)))
    cotangent = bell_draw(key_of[1], (MICRO, SEQS, LENGTH, D), 1.0, 6.0, ((1, 8), (2, 4)), jnp.float32)
    routes_keys = jax.random.split(jax.random.fold_in(key_of[2], 1), MICRO * SEQS * LENGTH // TOK_MB)
    routes_turns = jax.random.permutation(jax.random.fold_in(key_of[2], 3), MICRO * SEQS * LENGTH // TOK_MB)
    routes = jax.vmap(lambda own, number: routed_block(jax.random.fold_in(key_of[2], 2), own, number, TOK_MB, EXPERTS, 1, CAP, 0))(routes_keys, routes_turns).reshape((MICRO, SEQS, LENGTH, 1))
    prefix = with_ends(jax.random.randint(key_of[3], (MICRO, SEQS), 0, LENGTH + 1), jax.random.fold_in(key_of[3], 1), 0, LENGTH).astype(jnp.int32)
    qkv_weight = bell_draw(key_of[4], (D, 3 * D), (D // 2) ** -0.5, 0.25, ((0, 32),))
    mix_weight = bell_draw(key_of[5], (D, D), (D // 16) ** -0.5, 0.75, ((0, 32),))
    up_weight = bell_draw(key_of[6], (D, FF), D ** -0.5, 0.1875, ((0, 32),))
    down_weight = bell_draw(key_of[7], (FF, D), FF ** -0.5, 0.09375, ((0, 32),))
    dense_gain = jnp.clip(1.0 + 0.1 * jax.random.normal(key_of[8], (2, D), jnp.float32), 0.5, 1.5).astype(jnp.bfloat16)
    expert_up = bell_draw(key_of[9], (EXPERTS, 2, D, EFF), D ** -0.5, 0.1875, ((0, 8), (3, 4)))
    expert_down = bell_draw(key_of[10], (EXPERTS, 2, EFF, D), EFF ** -0.5, 0.09375, ((0, 8), (2, 4)))
    expert_gain = jnp.clip(1.0 + 0.1 * jax.random.normal(key_of[11], (EXPERTS, 2, D), jnp.float32), 0.5, 1.5).astype(jnp.bfloat16)
    centroids = bell_draw(key_of[12], (EXPERTS, D), (0.7 * D ** -0.5), 0.13085938, ((0, 8),))
    return dict(tokens=tokens, cotangent=cotangent, routes=routes, prefix=prefix, qkv_weight=qkv_weight, mix_weight=mix_weight, up_weight=up_weight, down_weight=down_weight, dense_gain=dense_gain, expert_up=expert_up, expert_down=expert_down, expert_gain=expert_gain, centroids=centroids)


eps = 1e-05
highest = lax.Precision.HIGHEST

@jax.custom_vjp
def low(v):
    return lax.optimization_barrier(v.astype(jnp.bfloat16)).astype(jnp.float32)

@jax.custom_vjp
def low_back(v):
    return v

def low_keep(v):
    return (low(v), None)

def low_pass(kept, grad):
    return (grad,)

def back_keep(v):
    return (v, None)

def back_low(kept, grad):
    return (low(grad),)
low.defvjp(low_keep, low_pass)
low_back.defvjp(back_keep, back_low)

def layer_norm(values, gain):
    centred = values - lax.optimization_barrier(jnp.mean(values, -1, keepdims=True))
    spread = lax.optimization_barrier(jnp.mean(centred * centred, -1, keepdims=True))
    return centred * lax.rsqrt(spread + eps) * gain

def matmul(left, right):
    return jnp.dot(left, right, precision=highest)

def gelu(values):
    return jax.nn.gelu(values, approximate=True)

def dense_block(inputs, lengths, w_qkv, w_mix, w_up, w_down, gains):
    groups, length, width = inputs.shape
    heads = width // HEAD_DIM
    normed = low(layer_norm(inputs, gains[0]))
    qkv = low(low_back(jnp.einsum('gld,de->gle', normed, w_qkv, precision=highest)))
    query = qkv[..., :width].reshape(groups, length, heads, HEAD_DIM)
    keys = qkv[..., width:2 * width].reshape(groups, length, heads, HEAD_DIM)
    values = qkv[..., 2 * width:].reshape(groups, length, heads, HEAD_DIM)
    scores = low_back(jnp.einsum('glhd,gmhd->ghlm', query, keys, precision=highest) * HEAD_DIM ** (-0.5))
    position = jnp.arange(length, dtype=jnp.int32)
    allowed = (position[None, None, :] <= position[None, :, None]) | (position[None, None, :] < lengths[:, None, None])
    scores = jnp.where(allowed[:, None], scores, -1e+30)
    probs = jax.nn.softmax(scores, -1)
    mixed = low(low_back(jnp.einsum('ghlm,gmhd->glhd', low(probs), values, precision=highest)))
    mixed = mixed.reshape(groups, length, width)
    attn = low_back(jnp.einsum('gld,de->gle', mixed, w_mix, precision=highest))
    resid = inputs + attn
    normed2 = low(layer_norm(resid, gains[1]))
    pre = low_back(jnp.einsum('gld,df->glf', normed2, w_up, precision=highest))
    hidden = low(gelu(pre))
    ffn = low_back(jnp.einsum('glf,fd->gld', hidden, w_down, precision=highest))
    return (resid + ffn, attn, ffn)

def expert_block(slots, gain, w_first, w_second, centroid):
    score = matmul(slots, centroid)
    state = slots
    for layer in range(2):
        normed = low(layer_norm(state, gain[layer]))
        pre = low_back(matmul(normed, w_first[layer]))
        hidden = low(gelu(pre))
        state = state + low_back(matmul(hidden, w_second[layer]))
    return low(low_back(jax.nn.sigmoid(score)[:, None] * state))

def slot_tables(routes):
    flat = routes.reshape(-1).astype(jnp.int32)
    count = flat.shape[0]
    blocks = count // TOK_MB
    onehot = (flat.reshape(blocks, TOK_MB)[:, :, None] == jnp.arange(EXPERTS, dtype=jnp.int32)[None, None, :]).astype(jnp.int32)
    rank = lax.optimization_barrier(jnp.sum((jnp.cumsum(onehot, 1) - 1) * onehot, 2)).reshape(-1)
    block_of = jnp.arange(count, dtype=jnp.int32) // TOK_MB
    slot_of_token = (flat * (blocks * CAP) + block_of * CAP + rank).astype(jnp.int32)
    token_of_slot = jnp.zeros((EXPERTS * blocks * CAP,), jnp.int32).at[slot_of_token].set(jnp.arange(count, dtype=jnp.int32))
    valid = jnp.zeros((EXPERTS * blocks * CAP,), jnp.float32).at[slot_of_token].set(1.0)
    return (slot_of_token, token_of_slot, valid, blocks * CAP)

def reference(tokens, cotangent, routes, prefix, qkv_weight, mix_weight, up_weight, down_weight, dense_gain, expert_up, expert_down, expert_gain, centroids):
    slot_of_token, token_of_slot, valid, per_expert = slot_tables(routes)
    count = MICRO * SEQS
    group = math.gcd(max(1, 4096 // LENGTH), count)
    lengths = prefix.reshape(count // group, group).astype(jnp.int32)

    def forward(inputs, w_qkv, w_mix, w_up, w_down, gains, ex_up, ex_down, ex_gain, cents):
        seq_groups = inputs.reshape(count // group, group, LENGTH, D)

        def group_step(carry, item):
            return (carry, dense_block(item[0], item[1], w_qkv, w_mix, w_up, w_down, gains))
        _, (after, attn, ffn) = lax.scan(jax.checkpoint(group_step), jnp.zeros((), jnp.float32), (seq_groups, lengths))
        after = after.reshape(-1, D)
        sent = low(low_back(after))
        slots = (sent[token_of_slot] * valid[:, None]).reshape(EXPERTS, per_expert, D)
        results = lax.map(jax.checkpoint(lambda item: expert_block(*item)), (slots, ex_gain, ex_up, ex_down, cents))
        gated = results.reshape(-1, D)[slot_of_token]
        return (after + gated, (attn, ffn, gated))
    floats = [a.astype(jnp.float32) for a in (tokens, qkv_weight, mix_weight, up_weight, down_weight, dense_gain, expert_up, expert_down, expert_gain, centroids)]
    final, pullback, extras = jax.vjp(forward, *floats, has_aux=True)
    grads = pullback(cotangent.reshape(-1, D).astype(jnp.float32))

    def root_mean(values):
        flat = values.reshape(MICRO, SEQS, -1)
        return jnp.sqrt(lax.optimization_barrier(jnp.mean(flat * flat, 2)))
    stats = jnp.stack([root_mean(final), root_mean(extras[0]), root_mean(extras[1]), root_mean(extras[2])])
    return (final.reshape(tokens.shape).astype(jnp.bfloat16), grads[0].reshape(tokens.shape), grads[1], grads[2], grads[3], grads[4], grads[5], grads[6], grads[7], grads[8], grads[9], stats)
```

```python
import jax
import jax.numpy as jnp
from jax import lax
from jax.sharding import PartitionSpec as P

HEAD_DIM = 64


eps = 1e-05


def layer_norm(values, gain):
    centred = values - jnp.mean(values, -1, keepdims=True)
    spread = jnp.mean(centred * centred, -1, keepdims=True)
    return centred * lax.rsqrt(spread + eps) * gain


def norm_back(values, gain, grads):
    _, pullback = jax.vjp(layer_norm, values, gain)
    return pullback(grads)


def gelu(values):
    return jax.nn.gelu(values, approximate=True)


def gelu_back(values, grads):
    _, pullback = jax.vjp(gelu, values)
    return pullback(grads)[0]


def contract_rows(left, right):
    return lax.dot_general(
        left, right, (((0,), (0,)), ((), ())), preferred_element_type=jnp.float32
    )


def contract_cols(left, right):
    return lax.dot_general(
        left, right, (((1,), (1,)), ((), ())), preferred_element_type=jnp.float32
    )


def swap(values, bit):
    count = lax.axis_size("expert")
    return lax.ppermute(values, "expert", [(i, i ^ bit) for i in range(count)])


def bit_orders():
    count = lax.axis_size("expert")
    bits = [1 << i for i in range(count.bit_length() - 1)]
    upper = bits[1:]
    half = len(upper) // 2
    return upper[half:] + upper[:half] + bits[:1], upper[:half] + upper[half:] + bits[:1]


def gather_rows(shard, order):
    count = lax.axis_size("expert")
    own = lax.axis_index("expert")
    pieces = [(0, lax.all_gather(shard, "dp", axis=0))]
    for bit in order:
        pieces = pieces + [(mask ^ bit, swap(piece, bit)) for mask, piece in pieces]
    dp_count, rows, cols = pieces[0][1].shape
    full = jnp.zeros((dp_count, count, rows, cols), shard.dtype)
    for mask, piece in pieces:
        full = lax.dynamic_update_slice_in_dim(full, piece[:, None], own ^ mask, 1)
    return full.reshape(dp_count * count * rows, cols)


def scatter_rows(total, order):
    count = lax.axis_size("expert")
    dp_count = lax.axis_size("dp")
    own = lax.axis_index("expert")
    rows = total.shape[0] // (count * dp_count)
    bits = sorted(order)
    current = total.reshape((dp_count,) + (2,) * len(bits) + (rows, total.shape[1]))
    left = sorted(bits, reverse=True)
    for bit in order:
        axis = 1 + left.index(bit)
        mine = (own // bit) % 2
        send = lax.dynamic_index_in_dim(current, 1 - mine, axis, keepdims=False)
        keep = lax.dynamic_index_in_dim(current, mine, axis, keepdims=False)
        received = swap(send, bit)
        current = (keep.astype(jnp.float32) + received.astype(jnp.float32)).astype(jnp.bfloat16)
        left.remove(bit)
    return lax.psum_scatter(
        current.reshape(dp_count * rows, -1), "dp", scatter_dimension=0, tiled=True
    ).astype(jnp.float32)


def spread_heads(blocks):
    return lax.all_to_all(blocks, "dp", split_axis=0, concat_axis=0, tiled=True)


def expert_forward(rows, gain, w_first, w_second, centroid):
    state = rows.astype(jnp.float32)
    score = jnp.dot(rows, centroid, preferred_element_type=jnp.float32)
    kept = []
    for layer in range(2):
        normed = layer_norm(state, gain[layer].astype(jnp.float32)).astype(jnp.bfloat16)
        gathered = lax.all_gather(normed, "dp", axis=0, tiled=True)
        pre = jnp.dot(gathered, w_first[layer], preferred_element_type=jnp.float32)
        hidden = gelu(pre).astype(jnp.bfloat16)
        partial_out = jnp.dot(hidden, w_second[layer], preferred_element_type=jnp.float32)
        added = lax.psum_scatter(
            partial_out.astype(jnp.bfloat16), "dp", scatter_dimension=0, tiled=True
        ).astype(jnp.float32)
        kept.append((state, gathered, pre, hidden))
        state = state + added
    gated = (jax.nn.sigmoid(score)[:, None] * state).astype(jnp.bfloat16)
    return (gated, (kept, state, score))


def expert_backward(grad_rows, rows, gain, w_first, w_second, centroid, saved):
    kept, state, score = saved
    incoming = grad_rows.astype(jnp.float32)
    sig = jax.nn.sigmoid(score)
    score_grad = jnp.sum(incoming * state, 1) * sig * (1.0 - sig)
    carried = incoming * sig[:, None]
    up_grads = [None, None]
    down_grads = [None, None]
    gain_grads = [None, None]
    for layer in (1, 0):
        before, gathered, pre, hidden = kept[layer]
        out_grad = lax.all_gather(carried.astype(jnp.bfloat16), "dp", axis=0, tiled=True)
        down_grads[layer] = contract_rows(hidden, out_grad)
        hidden_grad = contract_cols(out_grad, w_second[layer])
        pre_grad = gelu_back(pre, hidden_grad).astype(jnp.bfloat16)
        up_grads[layer] = contract_rows(gathered, pre_grad)
        normed_part = contract_cols(pre_grad, w_first[layer])
        normed_grad = lax.psum_scatter(
            normed_part.astype(jnp.bfloat16), "dp", scatter_dimension=0, tiled=True
        ).astype(jnp.float32)
        state_grad, gain_grad = norm_back(before, gain[layer].astype(jnp.float32), normed_grad)
        gain_grads[layer] = gain_grad
        carried = carried + state_grad
    input_grad = carried + score_grad[:, None] * centroid.astype(jnp.float32)[None, :]
    centroid_grad = jnp.sum(score_grad[:, None] * rows.astype(jnp.float32), 0)
    return (
        input_grad.astype(jnp.bfloat16),
        jnp.stack(up_grads),
        jnp.stack(down_grads),
        jnp.stack(gain_grads),
        centroid_grad,
    )


def shards(
    tokens,
    cotangent,
    routes,
    prefix,
    qkv_weight,
    mix_weight,
    up_weight,
    down_weight,
    dense_gain,
    expert_up,
    expert_down,
    expert_gain,
    centroids,
):
    micro_count, _, rows_dev, width = tokens.shape
    dp_count = lax.axis_size("dp")
    experts = lax.axis_size("expert")
    capacity = max(2, 5 * rows_dev // (4 * experts))
    length = rows_dev * dp_count
    heads = width // HEAD_DIM
    scale = HEAD_DIM ** (-0.5)
    key_pos = jnp.arange(length, dtype=jnp.int32)
    slot_ids = jnp.arange(experts * capacity, dtype=jnp.int32)
    expert_ids = jnp.arange(experts, dtype=jnp.int32)
    order_a, order_b = bit_orders()
    gain_cols = jnp.pad(dense_gain.T, ((0, 0), (0, 126)))
    half = qkv_weight.shape[1] // 2
    first_qkv = gather_rows(jnp.concatenate([qkv_weight[:, :half], gain_cols], 1), order_a)
    full_qkv = jnp.concatenate(
        [first_qkv[:, :half], gather_rows(qkv_weight[:, half:], order_b)], 1
    )
    full_gain = first_qkv[:, half : half + 2].T
    full_mix = gather_rows(mix_weight, order_a)
    full_up = gather_rows(up_weight, order_a)
    full_down = gather_rows(down_weight, order_b)
    gains = full_gain.astype(jnp.float32)

    def scores_of(query, keys, allowed):
        raw = jnp.einsum("thd,lhd->htl", query, keys, preferred_element_type=jnp.float32) * scale
        return jnp.where(allowed[None], raw, -1e30)

    stash = []
    stat_list = []
    output_list = []
    for micro in range(micro_count):
        inputs = tokens[micro, 0].astype(jnp.float32)
        normed = layer_norm(inputs, gains[0]).astype(jnp.bfloat16)
        qkv = jnp.dot(normed, full_qkv, preferred_element_type=jnp.float32).astype(jnp.bfloat16)
        mine = width // dp_count
        blocks = qkv.reshape(rows_dev, 3, dp_count, mine).transpose(2, 0, 1, 3)
        whole = spread_heads(blocks.reshape(dp_count, rows_dev, 3 * mine)).reshape(
            length, 3, heads // dp_count, HEAD_DIM
        )
        query, keys, values = (whole[:, 0], whole[:, 1], whole[:, 2])
        allowed = (key_pos[None, :] <= key_pos[:, None]) | (key_pos[None, :] < prefix[micro, 0])
        scores = scores_of(query, keys, allowed)
        row_max = jnp.max(scores, -1, keepdims=True)
        log_total = jnp.log(jnp.sum(jnp.exp(scores - row_max), -1, keepdims=True)) + row_max
        probs_low = jnp.exp(scores - log_total).astype(jnp.bfloat16)
        mixed = jnp.einsum("htl,lhd->thd", probs_low, values, preferred_element_type=jnp.float32)
        mixed = mixed.astype(jnp.bfloat16).reshape(dp_count, rows_dev, mine)
        mixed = spread_heads(mixed).transpose(1, 0, 2).reshape(rows_dev, width)
        attn = jnp.dot(mixed, full_mix, preferred_element_type=jnp.float32)
        resid = inputs + attn
        normed2 = layer_norm(resid, gains[1]).astype(jnp.bfloat16)
        pre = jnp.dot(normed2, full_up, preferred_element_type=jnp.float32)
        hidden = gelu(pre).astype(jnp.bfloat16)
        ffn = jnp.dot(hidden, full_down, preferred_element_type=jnp.float32)
        after = resid + ffn
        route = routes[micro, 0, :, 0]
        onehot = (route[:, None] == expert_ids[None, :]).astype(jnp.int32)
        rank = jnp.sum((jnp.cumsum(onehot, 0) - 1) * onehot, 1)
        slot = route * capacity + rank
        place = (slot[None, :] == slot_ids[:, None]).astype(jnp.bfloat16)
        sent = jnp.dot(
            place, after.astype(jnp.bfloat16), preferred_element_type=jnp.float32
        ).astype(jnp.bfloat16)
        rows = lax.all_to_all(
            sent.reshape(experts, capacity, width),
            "expert",
            split_axis=0,
            concat_axis=0,
            tiled=True,
        ).reshape(experts * capacity, width)
        gated, saved = expert_forward(
            rows, expert_gain[0], expert_up[0], expert_down[0], centroids[0]
        )
        returned = lax.all_to_all(
            gated.reshape(experts, capacity, width),
            "expert",
            split_axis=0,
            concat_axis=0,
            tiled=True,
        ).reshape(experts * capacity, width)
        branch = contract_rows(place, returned)
        final = after + branch
        output_list.append(final.astype(jnp.bfloat16))
        stat_list.append(
            jnp.stack(
                [
                    jnp.sum(final * final),
                    jnp.sum(attn * attn),
                    jnp.sum(ffn * ffn),
                    jnp.sum(branch * branch),
                ]
            )
        )
        stash.append(
            (
                inputs,
                normed,
                query,
                keys,
                values,
                allowed,
                log_total,
                mixed,
                resid,
                normed2,
                pre,
                hidden,
                place,
                rows,
                saved,
            )
        )
    back_qkv, back_mix, back_up, back_down, back_gains = (
        full_qkv,
        full_mix,
        full_up,
        full_down,
        gains,
    )
    ex_up_acc = jnp.zeros(expert_up.shape[1:], jnp.float32)
    ex_down_acc = jnp.zeros(expert_down.shape[1:], jnp.float32)
    ex_gain_acc = jnp.zeros((2, width), jnp.float32)
    cent_acc = jnp.zeros((width,), jnp.float32)
    gain_acc = jnp.zeros((2, width), jnp.float32)
    input_grads = []
    (
        normed_rows,
        qkv_grad_rows,
        mixed_rows,
        attn_rows,
        normed2_rows,
        pre_grad_rows,
        hidden_rows,
        ffn_rows,
    ) = ([], [], [], [], [], [], [], [])
    for micro in range(micro_count):
        (
            inputs,
            normed,
            query,
            keys,
            values,
            allowed,
            log_total,
            mixed,
            resid,
            normed2,
            pre,
            hidden,
            place,
            rows,
            saved,
        ) = stash[micro]
        upstream = cotangent[micro, 0]
        upstream_low = upstream.astype(jnp.bfloat16)
        grad_sent = jnp.dot(place, upstream_low, preferred_element_type=jnp.float32).astype(
            jnp.bfloat16
        )
        grad_rows = lax.all_to_all(
            grad_sent.reshape(experts, capacity, width),
            "expert",
            split_axis=0,
            concat_axis=0,
            tiled=True,
        ).reshape(experts * capacity, width)
        row_grad, up_part, down_part, gain_part, cent_part = expert_backward(
            grad_rows, rows, expert_gain[0], expert_up[0], expert_down[0], centroids[0], saved
        )
        ex_up_acc = ex_up_acc + up_part
        ex_down_acc = ex_down_acc + down_part
        ex_gain_acc = ex_gain_acc + gain_part
        cent_acc = cent_acc + cent_part
        grad_back = lax.all_to_all(
            row_grad.reshape(experts, capacity, width),
            "expert",
            split_axis=0,
            concat_axis=0,
            tiled=True,
        ).reshape(experts * capacity, width)
        after_grad = upstream + contract_rows(place, grad_back)
        ffn_low = after_grad.astype(jnp.bfloat16)
        hidden_grad = contract_cols(ffn_low, back_down)
        pre_grad = gelu_back(pre, hidden_grad).astype(jnp.bfloat16)
        normed2_grad = contract_cols(pre_grad, back_up)
        resid_part, gain2_grad = norm_back(resid, back_gains[1], normed2_grad)
        resid_grad = after_grad + resid_part
        attn_low = resid_grad.astype(jnp.bfloat16)
        mixed_grad = contract_cols(attn_low, back_mix).astype(jnp.bfloat16)
        mixed_grad = mixed_grad.reshape(rows_dev, dp_count, mine).transpose(1, 0, 2)
        mixed_grad = spread_heads(mixed_grad).reshape(length, heads // dp_count, HEAD_DIM)
        probs = jnp.exp(scores_of(query, keys, allowed) - log_total)
        probs_back = probs.astype(jnp.bfloat16)
        prob_grad = jnp.einsum(
            "thd,lhd->htl", mixed_grad, values, preferred_element_type=jnp.float32
        )
        inner = jnp.sum(probs * prob_grad, -1, keepdims=True)
        score_grad = (probs * (prob_grad - inner)).astype(jnp.bfloat16)
        query_grad = (
            jnp.einsum("htl,lhd->thd", score_grad, keys, preferred_element_type=jnp.float32) * scale
        )
        key_grad = (
            jnp.einsum("htl,thd->lhd", score_grad, query, preferred_element_type=jnp.float32)
            * scale
        )
        value_grad = jnp.einsum(
            "htl,thd->lhd", probs_back, mixed_grad, preferred_element_type=jnp.float32
        )
        own_grads = jnp.stack([query_grad, key_grad, value_grad], 1).astype(jnp.bfloat16)
        own_grads = spread_heads(own_grads.reshape(dp_count, rows_dev, 3 * mine))
        qkv_grad = own_grads.reshape(dp_count, rows_dev, 3, mine).transpose(1, 2, 0, 3)
        qkv_grad = qkv_grad.reshape(rows_dev, 3 * width)
        normed_grad = contract_cols(qkv_grad, back_qkv)
        input_part, gain1_grad = norm_back(inputs, back_gains[0], normed_grad)
        input_grads.append(resid_grad + input_part)
        gain_acc = gain_acc + jnp.stack([gain1_grad, gain2_grad])
        normed_rows.append(normed)
        qkv_grad_rows.append(qkv_grad)
        mixed_rows.append(mixed)
        attn_rows.append(attn_low)
        normed2_rows.append(normed2)
        pre_grad_rows.append(pre_grad)
        hidden_rows.append(hidden)
        ffn_rows.append(ffn_low)
    qkv_acc = contract_rows(jnp.concatenate(normed_rows, 0), jnp.concatenate(qkv_grad_rows, 0))
    mix_acc = contract_rows(jnp.concatenate(mixed_rows, 0), jnp.concatenate(attn_rows, 0))
    up_acc = contract_rows(jnp.concatenate(normed2_rows, 0), jnp.concatenate(pre_grad_rows, 0))
    down_acc = contract_rows(jnp.concatenate(hidden_rows, 0), jnp.concatenate(ffn_rows, 0))
    low = jnp.bfloat16
    order_c, order_d = (order_a[::-1], order_b[::-1])
    half = 3 * width // 2
    down_out = scatter_rows(down_acc.astype(low), order_c)
    up_out = scatter_rows(up_acc.astype(low), order_d)
    mix_out = scatter_rows(mix_acc.astype(low), order_d)
    qkv_low = qkv_acc.astype(low)
    qkv_out = jnp.concatenate(
        [scatter_rows(qkv_low[:, :half], order_c), scatter_rows(qkv_low[:, half:], order_d)], 1
    )
    gain_out = lax.psum_scatter(
        gain_acc, ("dp", "expert"), scatter_dimension=1, tiled=True
    )
    stat_sums, ex_gain_sum, cent_sum = lax.psum(
        (jnp.stack(stat_list, 1), ex_gain_acc, cent_acc), "dp"
    )
    branch_rms = jnp.sqrt(stat_sums / (length * width)).reshape(4, micro_count, 1)
    outputs = jnp.stack(output_list)[:, None]
    input_grad = jnp.stack(input_grads)[:, None]
    return (
        outputs,
        input_grad,
        qkv_out,
        mix_out,
        up_out,
        down_out,
        gain_out,
        ex_up_acc[None],
        ex_down_acc[None],
        ex_gain_sum[None],
        cent_sum[None],
        branch_rms,
    )


def solution(mesh):
    return jax.shard_map(
        shards,
        mesh=mesh,
        in_specs=(
            P(None, "expert", "dp", None),
            P(None, "expert", "dp", None),
            P(None, "expert", "dp", None),
            P(None, "expert"),
            P(("dp", "expert"), None),
            P(("dp", "expert"), None),
            P(("dp", "expert"), None),
            P(("dp", "expert"), None),
            P(None, ("dp", "expert")),
            P("expert", None, None, "dp"),
            P("expert", None, "dp", None),
            P("expert", None, None),
            P("expert", None),
        ),
        out_specs=(
            P(None, "expert", "dp", None),
            P(None, "expert", "dp", None),
            P(("dp", "expert"), None),
            P(("dp", "expert"), None),
            P(("dp", "expert"), None),
            P(("dp", "expert"), None),
            P(None, ("dp", "expert")),
            P("expert", None, None, "dp"),
            P("expert", None, "dp", None),
            P("expert", None, None),
            P("expert", None),
            P(None, None, "expert"),
        ),
        check_vma=False,
    )
```

```python
import functools

import jax
import jax.numpy as jnp
from jax import lax
from jax.experimental import pallas as pl
from jax.experimental.pallas import tpu as pltpu
from jax.sharding import PartitionSpec as P

HEAD_DIM = 64


eps = 1e-05


def layer_norm(values, gain):
    centred = values - jnp.mean(values, -1, keepdims=True)
    spread = jnp.mean(centred * centred, -1, keepdims=True)
    return centred * lax.rsqrt(spread + eps) * gain


def norm_back(values, gain, grads):
    _, pullback = jax.vjp(layer_norm, values, gain)
    return pullback(grads)


def gelu(values):
    return jax.nn.gelu(values, approximate=True)


def gelu_back(values, grads):
    _, pullback = jax.vjp(gelu, values)
    return pullback(grads)[0]


def contract_rows(left, right):
    return lax.dot_general(
        left, right, (((0,), (0,)), ((), ())), preferred_element_type=jnp.float32
    )


def contract_cols(left, right):
    return lax.dot_general(
        left, right, (((1,), (1,)), ((), ())), preferred_element_type=jnp.float32
    )


def swap(values, bit):
    count = lax.axis_size("expert")
    return lax.ppermute(values, "expert", [(i, i ^ bit) for i in range(count)])


def turn(values, shift):
    count = lax.axis_size("dp")
    return lax.ppermute(values, "dp", [(i, (i + shift) % count) for i in range(count)])


def sum_small(values):
    total = values
    for shift in range(1, lax.axis_size("dp")):
        total = total + turn(values, shift)
    return total


def bit_orders():
    count = lax.axis_size("expert")
    bits = [1 << i for i in range(count.bit_length() - 1)]
    upper = bits[1:]
    half = len(upper) // 2
    return upper[half:] + upper[:half] + bits[:1], upper[:half] + upper[half:] + bits[:1]


def assemble_kernel(masks, *refs):
    pieces, full, sems = refs[: len(masks)], refs[-2], refs[-1]
    own = lax.axis_index("expert")
    copies = []
    for i, mask in enumerate(masks):
        copies.append(
            pltpu.make_async_copy(pieces[i], full.at[:, jnp.bitwise_xor(own, mask)], sems.at[i])
        )
    for copy in copies:
        copy.start()
    for copy in copies:
        copy.wait()


def assemble(pieces):
    masks = [mask for mask, _ in pieces]
    arrays = [piece for _, piece in pieces]
    dp_count, rows, cols = arrays[0].shape
    full = pl.pallas_call(
        functools.partial(assemble_kernel, masks),
        out_shape=jax.ShapeDtypeStruct((dp_count, len(masks), rows, cols), arrays[0].dtype),
        in_specs=[pl.BlockSpec(memory_space=pl.ANY)] * len(masks),
        out_specs=pl.BlockSpec(memory_space=pl.ANY),
        scratch_shapes=[pltpu.SemaphoreType.DMA((len(masks),))],
        name="assemble",
    )(*arrays)
    return full.reshape(dp_count * len(masks) * rows, cols)


def spread(piece, order):
    pieces = [(0, piece)]
    for bit in order:
        pieces = pieces + [(mask ^ bit, swap(part, bit)) for mask, part in pieces]
    return pieces


def gather_dp(shard):
    return lax.all_gather(shard, "dp", axis=0)


def turn_gather(shard):
    count = lax.axis_size("dp")
    own = lax.axis_index("dp")
    full = jnp.zeros((count,) + shard.shape, shard.dtype)
    for shift in range(count):
        part = shard if shift == 0 else turn(shard, shift)
        full = lax.dynamic_update_slice_in_dim(full, part[None], (own - shift) % count, 0)
    return full


def scatter_rows(total, order):
    count = lax.axis_size("expert")
    dp_count = lax.axis_size("dp")
    own = lax.axis_index("expert")
    rows = total.shape[0] // (count * dp_count)
    bits = sorted(order)
    current = total.reshape((dp_count,) + (2,) * len(bits) + (rows, total.shape[1]))
    left = sorted(bits, reverse=True)
    for bit in order:
        axis = 1 + left.index(bit)
        mine = (own // bit) % 2
        send = lax.dynamic_index_in_dim(current, 1 - mine, axis, keepdims=False)
        keep = lax.dynamic_index_in_dim(current, mine, axis, keepdims=False)
        received = swap(send, bit)
        current = (keep.astype(jnp.float32) + received.astype(jnp.float32)).astype(jnp.bfloat16)
        left.remove(bit)
    return lax.psum_scatter(
        current.reshape(dp_count * rows, -1), "dp", scatter_dimension=0, tiled=True
    ).astype(jnp.float32)


def swap_heads(blocks):
    return lax.all_to_all(blocks, "dp", split_axis=0, concat_axis=0, tiled=True)


def swap_experts(slots):
    count = lax.axis_size("expert")
    blocks = slots.reshape(count, -1, slots.shape[1])
    return lax.all_to_all(blocks, "expert", split_axis=0, concat_axis=0, tiled=True).reshape(
        slots.shape
    )


def head_probs(x_ref, query, allowed, width, h):
    keys = x_ref[:, width + h * HEAD_DIM : width + (h + 1) * HEAD_DIM]
    values = x_ref[:, 2 * width + h * HEAD_DIM : 2 * width + (h + 1) * HEAD_DIM]
    scores = jnp.where(allowed, contract_cols(keys, query), -1e30)
    top = jnp.max(scores, 0, keepdims=True)
    weights = jnp.exp(scores - top)
    return keys, values, weights, jnp.sum(weights, 0, keepdims=True)


def allowed_pairs(length, block, start, prefix):
    key_pos = lax.broadcasted_iota(jnp.int32, (length, block), 0)
    query_pos = start + lax.broadcasted_iota(jnp.int32, (length, block), 1)
    return (key_pos <= query_pos) | (key_pos < prefix)


def attend_kernel(prefix_ref, x_ref, out_ref):
    block, width = out_ref.shape
    length = x_ref.shape[0]
    start = pl.multiple_of(pl.program_id(0) * block, block)
    allowed = allowed_pairs(length, block, start, prefix_ref[0])
    query = x_ref[pl.ds(start, block), :width]
    parts = []
    for h in range(width // HEAD_DIM):
        own = query[:, h * HEAD_DIM : (h + 1) * HEAD_DIM] * HEAD_DIM ** (-0.5)
        _, values, weights, total = head_probs(x_ref, own, allowed, width, h)
        parts.append(contract_rows(values, weights.astype(jnp.bfloat16)) * (1.0 / total))
    out_ref[...] = jnp.concatenate(parts, 0).T.astype(out_ref.dtype)


def attend(whole, prefix, block):
    length, cols = whole.shape
    width = cols // 3
    return pl.pallas_call(
        attend_kernel,
        out_shape=jax.ShapeDtypeStruct((length, width), whole.dtype),
        grid=(length // block,),
        in_specs=[
            pl.BlockSpec(memory_space=pltpu.SMEM),
            pl.BlockSpec((length, cols), lambda i: (0, 0)),
        ],
        out_specs=pl.BlockSpec((block, width), lambda i: (i, 0)),
        name="attend",
    )(prefix, whole)


def attend_back_kernel(prefix_ref, x_ref, grad_ref, out_ref, key_acc, value_acc):
    block, width = grad_ref.shape
    length = x_ref.shape[0]
    step = pl.program_id(0)
    start = pl.multiple_of(step * block, block)
    allowed = allowed_pairs(length, block, start, prefix_ref[0])
    query = x_ref[pl.ds(start, block), :width]
    heads = width // HEAD_DIM

    @pl.when(step == 0)
    def _():
        key_acc[...] = jnp.zeros_like(key_acc)
        value_acc[...] = jnp.zeros_like(value_acc)

    parts = []
    for h in range(heads):
        own = query[:, h * HEAD_DIM : (h + 1) * HEAD_DIM] * HEAD_DIM ** (-0.5)
        grad = grad_ref[:, h * HEAD_DIM : (h + 1) * HEAD_DIM]
        keys, values, weights, total = head_probs(x_ref, own, allowed, width, h)
        probs = weights * (1.0 / total)
        prob_grad = contract_cols(values, grad)
        inner = jnp.sum(probs * prob_grad, 0, keepdims=True)
        score_grad = (probs * (prob_grad - inner)).astype(jnp.bfloat16)
        value_acc[h] += jnp.dot(
            probs.astype(jnp.bfloat16), grad, preferred_element_type=jnp.float32
        )
        key_acc[h] += jnp.dot(score_grad, own, preferred_element_type=jnp.float32)
        parts.append(contract_rows(keys, score_grad) * HEAD_DIM ** (-0.5))
    out_ref[pl.ds(start, block), :width] = jnp.concatenate(parts, 0).T.astype(out_ref.dtype)

    @pl.when(step == pl.num_programs(0) - 1)
    def _():
        out_ref[:, width : 2 * width] = jnp.concatenate(
            [key_acc[h] for h in range(heads)], 1
        ).astype(out_ref.dtype)
        out_ref[:, 2 * width :] = jnp.concatenate(
            [value_acc[h] for h in range(heads)], 1
        ).astype(out_ref.dtype)


def attend_back(whole, grads, prefix, block):
    length, cols = whole.shape
    width = cols // 3
    heads = width // HEAD_DIM
    return pl.pallas_call(
        attend_back_kernel,
        out_shape=jax.ShapeDtypeStruct((length, cols), whole.dtype),
        grid=(length // block,),
        in_specs=[
            pl.BlockSpec(memory_space=pltpu.SMEM),
            pl.BlockSpec((length, cols), lambda i: (0, 0)),
            pl.BlockSpec((block, width), lambda i: (i, 0)),
        ],
        out_specs=pl.BlockSpec((length, cols), lambda i: (0, 0)),
        scratch_shapes=[
            pltpu.VMEM((heads, length, HEAD_DIM), jnp.float32),
            pltpu.VMEM((heads, length, HEAD_DIM), jnp.float32),
        ],
        name="attend_back",
    )(prefix, whole, grads)


def gather_slots(rows):
    return lax.all_gather(rows, "dp", axis=0, tiled=True)


def scatter_slots(partial_sums):
    return lax.psum_scatter(partial_sums, "dp", scatter_dimension=0, tiled=True)


def sum_slots(partial_sums):
    return gather_slots(scatter_slots(partial_sums))


def own_slots(values):
    count = lax.axis_size("dp")
    size = values.shape[0] // count
    return lax.dynamic_slice_in_dim(values, lax.axis_index("dp") * size, size, 0)


def shards(
    tokens,
    cotangent,
    routes,
    prefix,
    qkv_weight,
    mix_weight,
    up_weight,
    down_weight,
    dense_gain,
    expert_up,
    expert_down,
    expert_gain,
    centroids,
):
    f32, low = jnp.float32, jnp.bfloat16
    micro_count, _, rows_dev, width = tokens.shape
    dp_count = lax.axis_size("dp")
    experts = lax.axis_size("expert")
    capacity = max(2, 5 * rows_dev // (4 * experts))
    length = rows_dev * dp_count
    mine = width // dp_count
    block = min(256, length)
    micros = range(micro_count)
    slot_ids = jnp.arange(experts * capacity, dtype=jnp.int32)
    expert_ids = jnp.arange(experts, dtype=jnp.int32)
    up_ex, down_ex, centroid = (expert_up[0], expert_down[0], centroids[0])
    gain_ex = expert_gain[0].astype(f32)

    places, grad_slots, grad_rows = ([], [], [])
    for micro in micros:
        route = routes[micro, 0, :, 0]
        onehot = (route[:, None] == expert_ids[None, :]).astype(jnp.int32)
        rank = jnp.sum((jnp.cumsum(onehot, 0) - 1) * onehot, 1)
        slot = route * capacity + rank
        place = (slot[None, :] == slot_ids[:, None]).astype(low)
        places.append(place)
        grad_sent = jnp.dot(
            place, cotangent[micro, 0].astype(low), preferred_element_type=f32
        ).astype(low)
        grad_slots.append(swap_experts(grad_sent))

    order_a, order_b = bit_orders()
    rows_qkv = qkv_weight.shape[0]
    by_dest = (
        qkv_weight.reshape(rows_qkv, 3, dp_count, mine)
        .transpose(0, 2, 1, 3)
        .reshape(rows_qkv, 3 * width)
    )
    half = 3 * width // 2
    gain_cols = jnp.pad(dense_gain.T, ((0, 0), (0, 126)))
    first = turn_gather(jnp.concatenate([by_dest, gain_cols], 1))
    part_a = spread(first[:, :, :half], order_a)
    part_b = spread(first[:, :, half:], order_b)
    qkv_pieces = dict(part_b)
    full_qkv = assemble(
        [(mask, jnp.concatenate([piece, qkv_pieces[mask][:, :, :half]], 2)) for mask, piece in part_a]
    )
    full_gain = assemble([(mask, piece[:, :, half:]) for mask, piece in part_b])
    gains = full_gain[:, :2].T.astype(f32)
    tie, by_dp_mix, by_dp_up, by_dp_down = (
        None,
        gather_dp(mix_weight),
        gather_dp(up_weight),
        gather_dp(down_weight),
    )
    full_mix = assemble(spread(by_dp_mix, order_a))
    full_up = assemble(spread(by_dp_up, order_a))
    full_down = assemble(spread(by_dp_down, order_b))
    for micro in micros:
        grad_rows.append(gather_slots(grad_slots[micro]))

    dense = []
    slots_in = []
    for micro in micros:
        source = tokens[micro, 0]
        if micro > 0:
            source, _ = lax.optimization_barrier((source, dense[micro - 1][6]))
        inputs = source.astype(f32)
        normed = layer_norm(inputs, gains[0]).astype(low)
        qkv = jnp.dot(normed, full_qkv, preferred_element_type=f32).astype(low)
        blocks = qkv.reshape(rows_dev, dp_count, 3 * mine).transpose(1, 0, 2)
        whole = swap_heads(blocks).reshape(length, 3 * mine)
        mixed = attend(whole, prefix[micro], block).reshape(dp_count, rows_dev, mine)
        mixed = swap_heads(mixed).transpose(1, 0, 2).reshape(rows_dev, width)
        attn = jnp.dot(mixed, full_mix, preferred_element_type=f32)
        resid = inputs + attn
        normed2 = layer_norm(resid, gains[1]).astype(low)
        pre = jnp.dot(normed2, full_up, preferred_element_type=f32)
        hidden = gelu(pre).astype(low)
        ffn = jnp.dot(hidden, full_down, preferred_element_type=f32)
        after = resid + ffn
        sent = jnp.dot(places[micro], after.astype(low), preferred_element_type=f32).astype(low)
        dense.append((inputs, normed, whole, mixed, attn, resid, ffn, normed2, pre, hidden, after))
        slots_in.append(swap_experts(sent))

    own_in, *grad_rows = lax.optimization_barrier((slots_in[0], *grad_rows))
    slots_in[0] = own_in
    up_sum = [None, None]
    down_sum = [None, None]
    gain_one = jnp.zeros((width,), f32)
    state = []
    for micro in micros:
        rows = gather_slots(slots_in[micro])
        sig = jax.nn.sigmoid(jnp.dot(rows, centroid, preferred_element_type=f32))[:, None]
        state0 = rows.astype(f32)
        z0 = layer_norm(state0, gain_ex[0]).astype(low)
        pre0 = jnp.dot(z0, up_ex[0], preferred_element_type=f32)
        h0 = gelu(pre0).astype(low)
        out0 = jnp.dot(h0, down_ex[0], preferred_element_type=f32).astype(low)
        state1 = state0 + sum_slots(out0).astype(f32)
        z1 = layer_norm(state1, gain_ex[1]).astype(low)
        pre1 = jnp.dot(z1, up_ex[1], preferred_element_type=f32)
        h1 = gelu(pre1).astype(low)
        out1 = jnp.dot(h1, down_ex[1], preferred_element_type=f32).astype(low)
        state.append((rows, sig, z0, pre0, h0, state1, z1, pre1, h1, out1))

    own_grads = []
    for micro in micros:
        rows, sig, z0, pre0, h0, state1, z1, pre1, h1, out1 = state[micro]
        incoming = grad_rows[micro].astype(f32)
        score_part = jnp.sum(incoming * out1.astype(f32), 1)
        grad2 = incoming * sig
        grad_y = grad2.astype(low)
        pre_grad = gelu_back(pre1, contract_cols(grad_y, down_ex[1])).astype(low)
        normed_grad = sum_slots(contract_cols(pre_grad, up_ex[1]).astype(low)).astype(f32)
        down_part, up_part = (contract_rows(h1, grad_y), contract_rows(z1, pre_grad))
        down_sum[1] = down_part if micro == 0 else down_sum[1] + down_part
        up_sum[1] = up_part if micro == 0 else up_sum[1] + up_part
        state_grad, gain_grad = norm_back(state1, gain_ex[1], normed_grad)
        gain_one = gain_one + gain_grad
        grad1 = grad2 + state_grad
        grad_y = grad1.astype(low)
        pre_grad = gelu_back(pre0, contract_cols(grad_y, down_ex[0])).astype(low)
        normed_grad = scatter_slots(contract_cols(pre_grad, up_ex[0]).astype(low)).astype(f32)
        down_part, up_part = (contract_rows(h0, grad_y), contract_rows(z0, pre_grad))
        down_sum[0] = down_part if micro == 0 else down_sum[0] + down_part
        up_sum[0] = up_part if micro == 0 else up_sum[0] + up_part
        own_rows = own_slots(rows).astype(f32)
        state_grad, gain_grad = norm_back(own_rows, gain_ex[0], normed_grad)
        own_sig = own_slots(sig)[:, 0]
        score_grad = own_slots(sum_small(score_part)) + jnp.sum(
            own_slots(incoming) * own_slots(state1), 1
        )
        score_grad = score_grad * own_sig * (1.0 - own_sig)
        row_grad = own_slots(grad1) + state_grad + score_grad[:, None] * centroid.astype(f32)
        cent_grad = jnp.sum(score_grad[:, None] * own_rows, 0)
        own_grads.append((row_grad.astype(low), gain_grad, cent_grad, normed_grad))

    gain_acc = jnp.zeros((2, width), f32)
    input_grads = []
    kept = []
    for micro in micros:
        inputs, normed, whole, mixed, attn, resid, ffn, normed2, pre, hidden, after = dense[micro]
        grad_back = swap_experts(own_grads[micro][0])
        after_grad = cotangent[micro, 0] + contract_rows(places[micro], grad_back)
        ffn_low = after_grad.astype(low)
        hidden_grad = contract_cols(ffn_low, full_down)
        pre_grad = gelu_back(pre, hidden_grad).astype(low)
        normed2_grad = contract_cols(pre_grad, full_up)
        resid_part, gain2_grad = norm_back(resid, gains[1], normed2_grad)
        resid_grad = after_grad + resid_part
        attn_low = resid_grad.astype(low)
        mixed_grad = contract_cols(attn_low, full_mix).astype(low)
        mixed_grad = mixed_grad.reshape(rows_dev, dp_count, mine).transpose(1, 0, 2)
        mixed_grad = swap_heads(mixed_grad).reshape(length, mine)
        whole_grad = attend_back(whole, mixed_grad, prefix[micro], block)
        qkv_grad = swap_heads(whole_grad.reshape(dp_count, rows_dev, 3 * mine))
        qkv_grad = qkv_grad.transpose(1, 0, 2).reshape(rows_dev, 3 * width)
        normed_grad = contract_cols(qkv_grad, full_qkv)
        input_part, gain1_grad = norm_back(inputs, gains[0], normed_grad)
        input_grads.append(resid_grad + input_part)
        gain_acc = gain_acc + jnp.stack([gain1_grad, gain2_grad])
        kept.append((normed, qkv_grad, mixed, attn_low, normed2, pre_grad, hidden, ffn_low))
    joined = [jnp.concatenate(parts, 0) for parts in zip(*kept)]
    order_c, order_d = (order_a[::-1], order_b[::-1])
    down_out = scatter_rows(contract_rows(joined[6], joined[7]).astype(low), order_c)
    up_out = scatter_rows(contract_rows(joined[4], joined[5]).astype(low), order_d)
    mix_out = scatter_rows(contract_rows(joined[2], joined[3]).astype(low), order_d)
    qkv_low = contract_rows(joined[0], joined[1]).astype(low)
    qkv_out = jnp.concatenate(
        [scatter_rows(qkv_low[:, :half], order_c), scatter_rows(qkv_low[:, half:], order_d)], 1
    )
    qkv_out = (
        qkv_out.reshape(rows_qkv, dp_count, 3, mine)
        .transpose(0, 2, 1, 3)
        .reshape(rows_qkv, 3 * width)
    )

    output_list = []
    stat_list = []
    for micro in micros:
        rows, sig, state1, out1 = (state[micro][i] for i in (0, 1, 5, 9))
        attn, ffn, after = (dense[micro][i] for i in (4, 6, 10))
        late, _ = lax.optimization_barrier((out1, own_grads[-1][3]))
        state2 = own_slots(state1) + scatter_slots(late).astype(f32)
        returned = swap_experts((own_slots(sig) * state2).astype(low))
        branch = contract_rows(places[micro], returned)
        final = after + branch
        output_list.append(final.astype(low))
        stat_list.append(jnp.stack([jnp.sum(v * v) for v in (final, attn, ffn, branch)]))

    small = jnp.concatenate(
        [
            jnp.stack(stat_list, 1).reshape(-1),
            sum(part[1] for part in own_grads),
            sum(part[2] for part in own_grads),
        ]
    )
    small = sum_small(small)
    stats = 4 * micro_count
    branch_rms = jnp.sqrt(small[:stats] / (length * width)).reshape(4, micro_count, 1)
    ex_gain = jnp.stack([small[stats : stats + width], gain_one])
    gain_sum = sum_small(gain_acc)
    for bit in order_a:
        gain_sum = gain_sum + swap(gain_sum, bit)
    device = lax.axis_index("dp") * experts + lax.axis_index("expert")
    gain_out = lax.dynamic_index_in_dim(
        gain_sum.reshape(2, dp_count * experts, -1), device, 1, keepdims=False
    )
    return (
        jnp.stack(output_list)[:, None],
        jnp.stack(input_grads)[:, None],
        qkv_out,
        mix_out,
        up_out,
        down_out,
        gain_out,
        jnp.stack(up_sum)[None],
        jnp.stack(down_sum)[None],
        ex_gain[None],
        small[None, stats + width :],
        branch_rms,
    )


def solution(mesh):
    return jax.shard_map(
        shards,
        mesh=mesh,
        in_specs=(
            P(None, "expert", "dp", None),
            P(None, "expert", "dp", None),
            P(None, "expert", "dp", None),
            P(None, "expert"),
            P(("dp", "expert"), None),
            P(("dp", "expert"), None),
            P(("dp", "expert"), None),
            P(("dp", "expert"), None),
            P(None, ("dp", "expert")),
            P("expert", None, None, "dp"),
            P("expert", None, "dp", None),
            P("expert", None, None),
            P("expert", None),
        ),
        out_specs=(
            P(None, "expert", "dp", None),
            P(None, "expert", "dp", None),
            P(("dp", "expert"), None),
            P(("dp", "expert"), None),
            P(("dp", "expert"), None),
            P(("dp", "expert"), None),
            P(None, ("dp", "expert")),
            P("expert", None, None, "dp"),
            P("expert", None, "dp", None),
            P("expert", None, None),
            P("expert", None),
            P(None, None, "expert"),
        ),
        check_vma=False,
    )
```

```python
import functools

import jax
import jax.numpy as jnp
from jax import lax
from jax.experimental import pallas as pl
from jax.experimental.pallas import tpu as pltpu
from jax.sharding import PartitionSpec as P

HEAD_DIM = 64


eps = 1e-05


def layer_norm(values, gain):
    centred = values - jnp.mean(values, -1, keepdims=True)
    spread = jnp.mean(centred * centred, -1, keepdims=True)
    return centred * lax.rsqrt(spread + eps) * gain


def norm_back(values, gain, grads):
    _, pullback = jax.vjp(layer_norm, values, gain)
    return pullback(grads)


def gelu(values):
    return jax.nn.gelu(values, approximate=True)


def gelu_back(values, grads):
    _, pullback = jax.vjp(gelu, values)
    return pullback(grads)[0]


def contract_rows(left, right):
    return lax.dot_general(
        left, right, (((0,), (0,)), ((), ())), preferred_element_type=jnp.float32
    )


def contract_cols(left, right):
    return lax.dot_general(
        left, right, (((1,), (1,)), ((), ())), preferred_element_type=jnp.float32
    )


def swap(values, bit):
    count = lax.axis_size("expert")
    return lax.ppermute(values, "expert", [(i, i ^ bit) for i in range(count)])


def turn(values, shift):
    count = lax.axis_size("dp")
    return lax.ppermute(values, "dp", [(i, (i + shift) % count) for i in range(count)])


def sum_small(values):
    total = values
    for shift in range(1, lax.axis_size("dp")):
        total = total + turn(values, shift)
    return total


def bit_orders():
    count = lax.axis_size("expert")
    bits = [1 << i for i in range(count.bit_length() - 1)]
    upper = bits[1:]
    half = len(upper) // 2
    return upper[half:] + upper[:half] + bits[:1], upper[:half] + upper[half:] + bits[:1]


def assemble_kernel(masks, *refs):
    count = len(masks)
    pieces, full, held, in_sems, out_sems = (
        refs[:count],
        refs[count],
        refs[count + 1],
        refs[count + 2],
        refs[count + 3],
    )
    own = lax.axis_index("expert")
    loads = [pltpu.make_async_copy(pieces[i], held.at[i], in_sems.at[i]) for i in range(count)]
    stores = [
        pltpu.make_async_copy(
            held.at[i], full.at[:, jnp.bitwise_xor(own, mask)], out_sems.at[i]
        )
        for i, mask in enumerate(masks)
    ]
    for load in loads:
        load.start()
    for load, store in zip(loads, stores):
        load.wait()
        store.start()
    for store in stores:
        store.wait()


def assemble(pieces):
    masks = [mask for mask, _ in pieces]
    arrays = [piece for _, piece in pieces]
    dp_count, rows, cols = arrays[0].shape
    full = pl.pallas_call(
        functools.partial(assemble_kernel, masks),
        out_shape=jax.ShapeDtypeStruct((dp_count, len(masks), rows, cols), arrays[0].dtype),
        in_specs=[pl.BlockSpec(memory_space=pl.ANY)] * len(masks),
        out_specs=pl.BlockSpec(memory_space=pl.ANY),
        scratch_shapes=[
            pltpu.VMEM((len(masks), dp_count, rows, cols), arrays[0].dtype),
            pltpu.SemaphoreType.DMA((len(masks),)),
            pltpu.SemaphoreType.DMA((len(masks),)),
        ],
        name="assemble",
    )(*arrays)
    return full.reshape(dp_count * len(masks) * rows, cols)


def spread(piece, order):
    pieces = [(0, piece)]
    for bit in order:
        pieces = pieces + [(mask ^ bit, swap(part, bit)) for mask, part in pieces]
    return pieces


def gather_dp(shard):
    return lax.all_gather(shard, "dp", axis=0)


def turn_gather(shard):
    count = lax.axis_size("dp")
    own = lax.axis_index("dp")
    full = jnp.zeros((count,) + shard.shape, shard.dtype)
    for shift in range(count):
        part = shard if shift == 0 else turn(shard, shift)
        full = lax.dynamic_update_slice_in_dim(full, part[None], (own - shift) % count, 0)
    return full


def scatter_rows(total, order):
    count = lax.axis_size("expert")
    dp_count = lax.axis_size("dp")
    own = lax.axis_index("expert")
    rows = total.shape[0] // (count * dp_count)
    bits = sorted(order)
    current = total.reshape((dp_count,) + (2,) * len(bits) + (rows, total.shape[1]))
    left = sorted(bits, reverse=True)
    for bit in order:
        axis = 1 + left.index(bit)
        mine = (own // bit) % 2
        send = lax.dynamic_index_in_dim(current, 1 - mine, axis, keepdims=False)
        keep = lax.dynamic_index_in_dim(current, mine, axis, keepdims=False)
        received = swap(send, bit)
        current = (keep.astype(jnp.float32) + received.astype(jnp.float32)).astype(jnp.bfloat16)
        left.remove(bit)
    return lax.psum_scatter(
        current.reshape(dp_count * rows, -1), "dp", scatter_dimension=0, tiled=True
    ).astype(jnp.float32)


def swap_heads(blocks):
    return lax.all_to_all(blocks, "dp", split_axis=0, concat_axis=0, tiled=True)


def swap_experts(slots):
    count = lax.axis_size("expert")
    blocks = slots.reshape(count, -1, slots.shape[1])
    return lax.all_to_all(blocks, "expert", split_axis=0, concat_axis=0, tiled=True).reshape(
        slots.shape
    )


def head_probs(x_ref, query, allowed, width, h):
    keys = x_ref[:, width + h * HEAD_DIM : width + (h + 1) * HEAD_DIM]
    values = x_ref[:, 2 * width + h * HEAD_DIM : 2 * width + (h + 1) * HEAD_DIM]
    scores = jnp.where(allowed, contract_cols(keys, query), -1e30)
    top = jnp.max(scores, 0, keepdims=True)
    weights = jnp.exp(scores - top)
    return keys, values, weights, jnp.sum(weights, 0, keepdims=True)


def allowed_pairs(length, block, start, prefix):
    key_pos = lax.broadcasted_iota(jnp.int32, (length, block), 0)
    query_pos = start + lax.broadcasted_iota(jnp.int32, (length, block), 1)
    return (key_pos <= query_pos) | (key_pos < prefix)


def attend_kernel(prefix_ref, x_ref, out_ref):
    block, width = out_ref.shape
    length = x_ref.shape[0]
    start = pl.multiple_of(pl.program_id(0) * block, block)
    allowed = allowed_pairs(length, block, start, prefix_ref[0])
    query = x_ref[pl.ds(start, block), :width]
    parts = []
    for h in range(width // HEAD_DIM):
        own = query[:, h * HEAD_DIM : (h + 1) * HEAD_DIM] * HEAD_DIM ** (-0.5)
        _, values, weights, total = head_probs(x_ref, own, allowed, width, h)
        parts.append(contract_rows(values, weights.astype(jnp.bfloat16)) * (1.0 / total))
    out_ref[...] = jnp.concatenate(parts, 0).T.astype(out_ref.dtype)


def attend(whole, prefix, block):
    length, cols = whole.shape
    width = cols // 3
    return pl.pallas_call(
        attend_kernel,
        out_shape=jax.ShapeDtypeStruct((length, width), whole.dtype),
        grid=(length // block,),
        in_specs=[
            pl.BlockSpec(memory_space=pltpu.SMEM),
            pl.BlockSpec((length, cols), lambda i: (0, 0)),
        ],
        out_specs=pl.BlockSpec((block, width), lambda i: (i, 0)),
        name="attend",
    )(prefix, whole)


def attend_back_kernel(prefix_ref, x_ref, grad_ref, out_ref, key_acc, value_acc):
    block, width = grad_ref.shape
    length = x_ref.shape[0]
    step = pl.program_id(0)
    start = pl.multiple_of(step * block, block)
    allowed = allowed_pairs(length, block, start, prefix_ref[0])
    query = x_ref[pl.ds(start, block), :width]
    heads = width // HEAD_DIM

    @pl.when(step == 0)
    def _():
        key_acc[...] = jnp.zeros_like(key_acc)
        value_acc[...] = jnp.zeros_like(value_acc)

    parts = []
    for h in range(heads):
        own = query[:, h * HEAD_DIM : (h + 1) * HEAD_DIM] * HEAD_DIM ** (-0.5)
        grad = grad_ref[:, h * HEAD_DIM : (h + 1) * HEAD_DIM]
        keys, values, weights, total = head_probs(x_ref, own, allowed, width, h)
        probs = weights * (1.0 / total)
        prob_grad = contract_cols(values, grad)
        inner = jnp.sum(probs * prob_grad, 0, keepdims=True)
        score_grad = (probs * (prob_grad - inner)).astype(jnp.bfloat16)
        value_acc[h] += jnp.dot(
            probs.astype(jnp.bfloat16), grad, preferred_element_type=jnp.float32
        )
        key_acc[h] += jnp.dot(score_grad, own, preferred_element_type=jnp.float32)
        parts.append(contract_rows(keys, score_grad) * HEAD_DIM ** (-0.5))
    out_ref[pl.ds(start, block), :width] = jnp.concatenate(parts, 0).T.astype(out_ref.dtype)

    @pl.when(step == pl.num_programs(0) - 1)
    def _():
        out_ref[:, width : 2 * width] = jnp.concatenate(
            [key_acc[h] for h in range(heads)], 1
        ).astype(out_ref.dtype)
        out_ref[:, 2 * width :] = jnp.concatenate(
            [value_acc[h] for h in range(heads)], 1
        ).astype(out_ref.dtype)


def attend_back(whole, grads, prefix, block):
    length, cols = whole.shape
    width = cols // 3
    heads = width // HEAD_DIM
    return pl.pallas_call(
        attend_back_kernel,
        out_shape=jax.ShapeDtypeStruct((length, cols), whole.dtype),
        grid=(length // block,),
        in_specs=[
            pl.BlockSpec(memory_space=pltpu.SMEM),
            pl.BlockSpec((length, cols), lambda i: (0, 0)),
            pl.BlockSpec((block, width), lambda i: (i, 0)),
        ],
        out_specs=pl.BlockSpec((length, cols), lambda i: (0, 0)),
        scratch_shapes=[
            pltpu.VMEM((heads, length, HEAD_DIM), jnp.float32),
            pltpu.VMEM((heads, length, HEAD_DIM), jnp.float32),
        ],
        name="attend_back",
    )(prefix, whole, grads)


def after(value, *others):
    return lax.optimization_barrier((value,) + others)[0]


def gather_slots(rows):
    return lax.all_gather(rows, "dp", axis=0, tiled=True)


def scatter_slots(partial_sums):
    return lax.psum_scatter(partial_sums, "dp", scatter_dimension=0, tiled=True)


def sum_slots(partial_sums):
    return gather_slots(scatter_slots(partial_sums))


def own_slots(values):
    count = lax.axis_size("dp")
    size = values.shape[0] // count
    return lax.dynamic_slice_in_dim(values, lax.axis_index("dp") * size, size, 0)


def shards(
    tokens,
    cotangent,
    routes,
    prefix,
    qkv_weight,
    mix_weight,
    up_weight,
    down_weight,
    dense_gain,
    expert_up,
    expert_down,
    expert_gain,
    centroids,
):
    f32, low = jnp.float32, jnp.bfloat16
    micro_count, _, rows_dev, width = tokens.shape
    dp_count = lax.axis_size("dp")
    experts = lax.axis_size("expert")
    capacity = max(2, 5 * rows_dev // (4 * experts))
    length = rows_dev * dp_count
    mine = width // dp_count
    block = min(256, length)
    micros = range(micro_count)
    slot_ids = jnp.arange(experts * capacity, dtype=jnp.int32)
    expert_ids = jnp.arange(experts, dtype=jnp.int32)
    up_ex, down_ex, centroid = (expert_up[0], expert_down[0], centroids[0])
    gain_ex = expert_gain[0].astype(f32)

    places, grad_slots, grad_rows = ([], [], [])
    for micro in micros:
        route = routes[micro, 0, :, 0]
        onehot = (route[:, None] == expert_ids[None, :]).astype(jnp.int32)
        rank = jnp.sum((jnp.cumsum(onehot, 0) - 1) * onehot, 1)
        slot = route * capacity + rank
        place = (slot[None, :] == slot_ids[:, None]).astype(low)
        places.append(place)
        grad_sent = jnp.dot(
            place, cotangent[micro, 0].astype(low), preferred_element_type=f32
        ).astype(low)
        grad_slots.append(swap_experts(grad_sent))

    order_a, order_b = bit_orders()
    rows_qkv = qkv_weight.shape[0]
    by_dest = (
        qkv_weight.reshape(rows_qkv, 3, dp_count, mine)
        .transpose(0, 2, 1, 3)
        .reshape(rows_qkv, 3 * width)
    )
    half = 3 * width // 2
    gain_cols = jnp.pad(dense_gain.T, ((0, 0), (0, 126)))
    first = turn_gather(jnp.concatenate([by_dest, gain_cols], 1))
    part_a = spread(first[:, :, :half], order_a)
    part_b = spread(first[:, :, half:], order_b)
    qkv_pieces = dict(part_b)
    full_qkv = assemble(
        [(mask, jnp.concatenate([piece, qkv_pieces[mask][:, :, :half]], 2)) for mask, piece in part_a]
    )
    full_gain = assemble([(mask, piece[:, :, half:]) for mask, piece in part_b])
    gains = full_gain[:, :2].T.astype(f32)
    full_mix = assemble(spread(turn_gather(mix_weight), order_a))
    full_up = assemble(spread(gather_dp(up_weight), order_a))
    full_down = assemble(spread(gather_dp(down_weight), order_b))
    for micro in micros:
        grad_rows.append(gather_slots(grad_slots[micro]))

    dense = []
    slots_in = []
    for micro in micros:
        source = tokens[micro, 0]
        if micro > 0:
            source = after(source, slots_in[micro - 1])
        inputs = source.astype(f32)
        normed = layer_norm(inputs, gains[0]).astype(low)
        qkv = jnp.dot(normed, full_qkv, preferred_element_type=f32).astype(low)
        blocks = qkv.reshape(rows_dev, dp_count, 3 * mine).transpose(1, 0, 2)
        whole = swap_heads(blocks).reshape(length, 3 * mine)
        mixed = attend(whole, prefix[micro], block).reshape(dp_count, rows_dev, mine)
        mixed = swap_heads(mixed).transpose(1, 0, 2).reshape(rows_dev, width)
        attn = jnp.dot(mixed, full_mix, preferred_element_type=f32)
        resid = inputs + attn
        normed2 = layer_norm(resid, gains[1]).astype(low)
        pre = jnp.dot(normed2, full_up, preferred_element_type=f32)
        hidden = gelu(pre).astype(low)
        ffn = jnp.dot(hidden, full_down, preferred_element_type=f32)
        dense_out = resid + ffn
        sent = jnp.dot(places[micro], dense_out.astype(low), preferred_element_type=f32).astype(low)
        dense.append((inputs, normed, whole, mixed, attn, resid, ffn, normed2, pre, hidden, dense_out))
        slots_in.append(swap_experts(sent))

    own_in, *grad_rows = lax.optimization_barrier((slots_in[0], *grad_rows))
    slots_in[0] = own_in
    up_sum = [None, None]
    down_sum = [None, None]
    gain_one = jnp.zeros((width,), f32)

    first_stage = []
    for micro in micros:
        rows = gather_slots(slots_in[micro])
        if micro > 0:
            rows = after(rows, first_stage[micro - 1][-1])
        sig = jax.nn.sigmoid(jnp.dot(rows, centroid, preferred_element_type=f32))[:, None]
        state0 = rows.astype(f32)
        z0 = layer_norm(state0, gain_ex[0]).astype(low)
        pre0 = jnp.dot(z0, up_ex[0], preferred_element_type=f32)
        h0 = gelu(pre0).astype(low)
        out0 = jnp.dot(h0, down_ex[0], preferred_element_type=f32).astype(low)
        first_stage.append((rows, sig, z0, pre0, h0, out0))
    summed0 = [sum_slots(first_stage[micro][-1]) for micro in micros]
    second_stage = []
    for micro in micros:
        rows, sig = first_stage[micro][:2]
        total = summed0[micro]
        if micro > 0:
            total = after(total, second_stage[micro - 1][-1])
        state1 = rows.astype(f32) + total.astype(f32)
        z1 = layer_norm(state1, gain_ex[1]).astype(low)
        pre1 = jnp.dot(z1, up_ex[1], preferred_element_type=f32)
        h1 = gelu(pre1).astype(low)
        out1 = jnp.dot(h1, down_ex[1], preferred_element_type=f32).astype(low)
        incoming = grad_rows[micro].astype(f32)
        score_part = jnp.sum(incoming * out1.astype(f32), 1)
        grad2 = incoming * sig
        grad_y = grad2.astype(low)
        pre_grad = gelu_back(pre1, contract_cols(grad_y, down_ex[1])).astype(low)
        normed_part = contract_cols(pre_grad, up_ex[1]).astype(low)
        second_stage.append(
            (state1, out1, incoming, score_part, grad2, z1, h1, grad_y, pre_grad, normed_part)
        )
    summed1 = [sum_slots(second_stage[micro][-1]) for micro in micros]
    third_stage = []
    for micro in micros:
        rows, sig, z0, pre0, h0, _ = first_stage[micro]
        state1, _, _, _, grad2, z1, h1, grad_y1, pre_grad1, _ = second_stage[micro]
        total = summed1[micro]
        if micro > 0:
            total = after(total, third_stage[micro - 1][-1])
        state_grad, gain_grad = norm_back(state1, gain_ex[1], total.astype(f32))
        gain_one = gain_one + gain_grad
        grad1 = grad2 + state_grad
        grad_y = grad1.astype(low)
        pre_grad = gelu_back(pre0, contract_cols(grad_y, down_ex[0])).astype(low)
        normed_part = contract_cols(pre_grad, up_ex[0]).astype(low)
        down_part, up_part = (contract_rows(h1, grad_y1), contract_rows(z1, pre_grad1))
        down_sum[1] = down_part if micro == 0 else down_sum[1] + down_part
        up_sum[1] = up_part if micro == 0 else up_sum[1] + up_part
        down_part, up_part = (contract_rows(h0, grad_y), contract_rows(z0, pre_grad))
        down_sum[0] = down_part if micro == 0 else down_sum[0] + down_part
        up_sum[0] = up_part if micro == 0 else up_sum[0] + up_part
        third_stage.append((grad1, normed_part))
    own_grads = []
    for micro in micros:
        rows, sig = first_stage[micro][:2]
        state1, _, incoming, score_part = second_stage[micro][:4]
        grad1, normed_part = third_stage[micro]
        normed_grad = scatter_slots(normed_part).astype(f32)
        own_rows = own_slots(rows).astype(f32)
        state_grad, gain_grad = norm_back(own_rows, gain_ex[0], normed_grad)
        own_sig = own_slots(sig)[:, 0]
        score_grad = own_slots(sum_small(score_part)) + jnp.sum(
            own_slots(incoming) * own_slots(state1), 1
        )
        score_grad = score_grad * own_sig * (1.0 - own_sig)
        row_grad = own_slots(grad1) + state_grad + score_grad[:, None] * centroid.astype(f32)
        cent_grad = jnp.sum(score_grad[:, None] * own_rows, 0)
        own_grads.append((row_grad.astype(low), gain_grad, cent_grad, normed_grad))

    gain_acc = jnp.zeros((2, width), f32)
    input_grads = []
    kept = []
    for micro in micros:
        inputs, normed, whole, mixed, attn, resid, ffn, normed2, pre, hidden, _ = dense[micro]
        grad_back = swap_experts(own_grads[micro][0])
        after_grad = cotangent[micro, 0] + contract_rows(places[micro], grad_back)
        ffn_low = after_grad.astype(low)
        hidden_grad = contract_cols(ffn_low, full_down)
        pre_grad = gelu_back(pre, hidden_grad).astype(low)
        normed2_grad = contract_cols(pre_grad, full_up)
        resid_part, gain2_grad = norm_back(resid, gains[1], normed2_grad)
        resid_grad = after_grad + resid_part
        attn_low = resid_grad.astype(low)
        mixed_grad = contract_cols(attn_low, full_mix).astype(low)
        mixed_grad = mixed_grad.reshape(rows_dev, dp_count, mine).transpose(1, 0, 2)
        mixed_grad = swap_heads(mixed_grad).reshape(length, mine)
        whole_grad = attend_back(whole, mixed_grad, prefix[micro], block)
        qkv_grad = swap_heads(whole_grad.reshape(dp_count, rows_dev, 3 * mine))
        qkv_grad = qkv_grad.transpose(1, 0, 2).reshape(rows_dev, 3 * width)
        normed_grad = contract_cols(qkv_grad, full_qkv)
        input_part, gain1_grad = norm_back(inputs, gains[0], normed_grad)
        input_grads.append(resid_grad + input_part)
        gain_acc = gain_acc + jnp.stack([gain1_grad, gain2_grad])
        kept.append((normed, qkv_grad, mixed, attn_low, normed2, pre_grad, hidden, ffn_low))
    joined = [jnp.concatenate(parts, 0) for parts in zip(*kept)]
    order_c, order_d = (order_a[::-1], order_b[::-1])
    down_out = scatter_rows(contract_rows(joined[6], joined[7]).astype(low), order_c)
    up_out = scatter_rows(contract_rows(joined[4], joined[5]).astype(low), order_d)
    mix_out = scatter_rows(contract_rows(joined[2], joined[3]).astype(low), order_d)
    qkv_low = contract_rows(joined[0], joined[1]).astype(low)
    qkv_out = jnp.concatenate(
        [scatter_rows(qkv_low[:, :half], order_c), scatter_rows(qkv_low[:, half:], order_d)], 1
    )
    qkv_out = (
        qkv_out.reshape(rows_qkv, dp_count, 3, mine)
        .transpose(0, 2, 1, 3)
        .reshape(rows_qkv, 3 * width)
    )

    output_list = []
    stat_list = []
    for micro in micros:
        sig = first_stage[micro][1]
        state1, out1 = second_stage[micro][:2]
        attn, ffn, dense_out = (dense[micro][i] for i in (4, 6, 10))
        late = scatter_slots(after(out1, own_grads[-1][3]))
        state2 = own_slots(state1) + after(late, kept[-1][1]).astype(f32)
        returned = swap_experts((own_slots(sig) * state2).astype(low))
        branch = contract_rows(places[micro], returned)
        final = dense_out + branch
        output_list.append(final.astype(low))
        stat_list.append(jnp.stack([jnp.sum(v * v) for v in (final, attn, ffn, branch)]))

    small = jnp.concatenate(
        [
            jnp.stack(stat_list, 1).reshape(-1),
            sum(part[1] for part in own_grads),
            sum(part[2] for part in own_grads),
        ]
    )
    small = sum_small(small)
    stats = 4 * micro_count
    branch_rms = jnp.sqrt(small[:stats] / (length * width)).reshape(4, micro_count, 1)
    ex_gain = jnp.stack([small[stats : stats + width], gain_one])
    gain_sum = sum_small(gain_acc)
    for bit in order_a:
        gain_sum = gain_sum + swap(gain_sum, bit)
    device = lax.axis_index("dp") * experts + lax.axis_index("expert")
    gain_out = lax.dynamic_index_in_dim(
        gain_sum.reshape(2, dp_count * experts, -1), device, 1, keepdims=False
    )
    return (
        jnp.stack(output_list)[:, None],
        jnp.stack(input_grads)[:, None],
        qkv_out,
        mix_out,
        up_out,
        down_out,
        gain_out,
        jnp.stack(up_sum)[None],
        jnp.stack(down_sum)[None],
        ex_gain[None],
        small[None, stats + width :],
        branch_rms,
    )


def solution(mesh):
    return jax.shard_map(
        shards,
        mesh=mesh,
        in_specs=(
            P(None, "expert", "dp", None),
            P(None, "expert", "dp", None),
            P(None, "expert", "dp", None),
            P(None, "expert"),
            P(("dp", "expert"), None),
            P(("dp", "expert"), None),
            P(("dp", "expert"), None),
            P(("dp", "expert"), None),
            P(None, ("dp", "expert")),
            P("expert", None, None, "dp"),
            P("expert", None, "dp", None),
            P("expert", None, None),
            P("expert", None),
        ),
        out_specs=(
            P(None, "expert", "dp", None),
            P(None, "expert", "dp", None),
            P(("dp", "expert"), None),
            P(("dp", "expert"), None),
            P(("dp", "expert"), None),
            P(("dp", "expert"), None),
            P(None, ("dp", "expert")),
            P("expert", None, None, "dp"),
            P("expert", None, "dp", None),
            P("expert", None, None),
            P("expert", None),
            P(None, None, "expert"),
        ),
        check_vma=False,
    )
```

```python
import functools

import jax
import jax.numpy as jnp
from jax import lax
from jax.experimental import pallas as pl
from jax.experimental.pallas import tpu as pltpu
from jax.sharding import PartitionSpec as P

HEAD_DIM = 64


eps = 1e-05


def layer_norm(values, gain):
    centred = values - jnp.mean(values, -1, keepdims=True)
    spread = jnp.mean(centred * centred, -1, keepdims=True)
    return centred * lax.rsqrt(spread + eps) * gain


def norm_back(values, gain, grads):
    _, pullback = jax.vjp(layer_norm, values, gain)
    return pullback(grads)


def gelu(values):
    return jax.nn.gelu(values, approximate=True)


def gelu_back(values, grads):
    _, pullback = jax.vjp(gelu, values)
    return pullback(grads)[0]


def contract_rows(left, right):
    return lax.dot_general(
        left, right, (((0,), (0,)), ((), ())), preferred_element_type=jnp.float32
    )


def contract_cols(left, right):
    return lax.dot_general(
        left, right, (((1,), (1,)), ((), ())), preferred_element_type=jnp.float32
    )


def swap(values, bit):
    count = lax.axis_size("expert")
    return lax.ppermute(values, "expert", [(i, i ^ bit) for i in range(count)])


def turn(values, shift):
    count = lax.axis_size("dp")
    return lax.ppermute(values, "dp", [(i, (i + shift) % count) for i in range(count)])


def sum_small(values):
    total = values
    for shift in range(1, lax.axis_size("dp")):
        total = total + turn(values, shift)
    return total


def bit_orders():
    count = lax.axis_size("expert")
    bits = [1 << i for i in range(count.bit_length() - 1)]
    upper = bits[1:]
    half = len(upper) // 2
    return upper[half:] + upper[:half] + bits[:1], upper[:half] + upper[half:] + bits[:1]


def assemble_kernel(masks, *refs):
    count = len(masks)
    pieces, full, held, in_sems, out_sems = (
        refs[:count],
        refs[count],
        refs[count + 1],
        refs[count + 2],
        refs[count + 3],
    )
    own = lax.axis_index("expert")
    loads = [pltpu.make_async_copy(pieces[i], held.at[i], in_sems.at[i]) for i in range(count)]
    stores = [
        pltpu.make_async_copy(
            held.at[i], full.at[:, jnp.bitwise_xor(own, mask)], out_sems.at[i]
        )
        for i, mask in enumerate(masks)
    ]
    for load in loads:
        load.start()
    for load, store in zip(loads, stores):
        load.wait()
        store.start()
    for store in stores:
        store.wait()


def assemble(pieces):
    masks = [mask for mask, _ in pieces]
    arrays = [piece for _, piece in pieces]
    dp_count, rows, cols = arrays[0].shape
    full = pl.pallas_call(
        functools.partial(assemble_kernel, masks),
        out_shape=jax.ShapeDtypeStruct((dp_count, len(masks), rows, cols), arrays[0].dtype),
        in_specs=[pl.BlockSpec(memory_space=pl.ANY)] * len(masks),
        out_specs=pl.BlockSpec(memory_space=pl.ANY),
        scratch_shapes=[
            pltpu.VMEM((len(masks), dp_count, rows, cols), arrays[0].dtype),
            pltpu.SemaphoreType.DMA((len(masks),)),
            pltpu.SemaphoreType.DMA((len(masks),)),
        ],
        name="assemble",
    )(*arrays)
    return full.reshape(dp_count * len(masks) * rows, cols)


def spread(piece, order):
    pieces = [(0, piece)]
    for bit in order:
        pieces = pieces + [(mask ^ bit, swap(part, bit)) for mask, part in pieces]
    return pieces


def gather_dp(shard):
    return lax.all_gather(shard, "dp", axis=0)


def turn_gather(shard):
    count = lax.axis_size("dp")
    own = lax.axis_index("dp")
    full = jnp.zeros((count,) + shard.shape, shard.dtype)
    for shift in range(count):
        part = shard if shift == 0 else turn(shard, shift)
        full = lax.dynamic_update_slice_in_dim(full, part[None], (own - shift) % count, 0)
    return full


def scatter_start(total, order):
    count = lax.axis_size("expert")
    dp_count = lax.axis_size("dp")
    rows = total.shape[0] // (count * dp_count)
    bits = sorted(order)
    current = total.reshape((dp_count,) + (2,) * len(bits) + (rows, total.shape[1]))
    left = sorted(bits, reverse=True)
    return scatter_bits(current, order[:1], left), order[1:], left


def scatter_bits(current, order, left):
    own = lax.axis_index("expert")
    for bit in order:
        axis = 1 + left.index(bit)
        mine = (own // bit) % 2
        send = lax.dynamic_index_in_dim(current, 1 - mine, axis, keepdims=False)
        keep = lax.dynamic_index_in_dim(current, mine, axis, keepdims=False)
        received = swap(send, bit)
        current = (keep.astype(jnp.float32) + received.astype(jnp.float32)).astype(jnp.bfloat16)
        left.remove(bit)
    return current


def scatter_end(started):
    current, order, left = started
    current = scatter_bits(current, order, left)
    return lax.psum_scatter(
        current.reshape(-1, current.shape[-1]), "dp", scatter_dimension=0, tiled=True
    ).astype(jnp.float32)


def scatter_rows(total, order):
    return scatter_end(scatter_start(total, order))


def swap_heads(blocks):
    return lax.all_to_all(blocks, "dp", split_axis=0, concat_axis=0, tiled=True)


def swap_experts(slots):
    count = lax.axis_size("expert")
    blocks = slots.reshape(count, -1, slots.shape[1])
    return lax.all_to_all(blocks, "expert", split_axis=0, concat_axis=0, tiled=True).reshape(
        slots.shape
    )


def head_probs(x_ref, query, allowed, width, h):
    keys = x_ref[:, width + h * HEAD_DIM : width + (h + 1) * HEAD_DIM]
    values = x_ref[:, 2 * width + h * HEAD_DIM : 2 * width + (h + 1) * HEAD_DIM]
    scores = jnp.where(allowed, contract_cols(keys, query), -1e30)
    top = jnp.max(scores, 0, keepdims=True)
    weights = jnp.exp(scores - top)
    return keys, values, weights, jnp.sum(weights, 0, keepdims=True)


def allowed_pairs(length, block, start, prefix):
    key_pos = lax.broadcasted_iota(jnp.int32, (length, block), 0)
    query_pos = start + lax.broadcasted_iota(jnp.int32, (length, block), 1)
    return (key_pos <= query_pos) | (key_pos < prefix)


def attend_kernel(prefix_ref, x_ref, out_ref):
    block, width = out_ref.shape
    length = x_ref.shape[0]
    start = pl.multiple_of(pl.program_id(0) * block, block)
    allowed = allowed_pairs(length, block, start, prefix_ref[0])
    query = x_ref[pl.ds(start, block), :width]
    parts = []
    for h in range(width // HEAD_DIM):
        own = query[:, h * HEAD_DIM : (h + 1) * HEAD_DIM] * HEAD_DIM ** (-0.5)
        _, values, weights, total = head_probs(x_ref, own, allowed, width, h)
        parts.append(contract_rows(values, weights.astype(jnp.bfloat16)) * (1.0 / total))
    out_ref[...] = jnp.concatenate(parts, 0).T.astype(out_ref.dtype)


def attend_cost(length, cols, products):
    return pl.CostEstimate(
        flops=products * length * length * cols // 3,
        transcendentals=length * length * cols // (3 * HEAD_DIM),
        bytes_accessed=products * length * cols,
    )


def attend(whole, prefix, block):
    length, cols = whole.shape
    width = cols // 3
    return pl.pallas_call(
        attend_kernel,
        out_shape=jax.ShapeDtypeStruct((length, width), whole.dtype),
        grid=(length // block,),
        in_specs=[
            pl.BlockSpec(memory_space=pltpu.SMEM),
            pl.BlockSpec((length, cols), lambda i: (0, 0)),
        ],
        out_specs=pl.BlockSpec((block, width), lambda i: (i, 0)),
        cost_estimate=attend_cost(length, cols, 4),
        name="attend",
    )(prefix, whole)


def attend_back_kernel(prefix_ref, x_ref, grad_ref, out_ref, key_acc, value_acc):
    block, width = grad_ref.shape
    length = x_ref.shape[0]
    step = pl.program_id(0)
    start = pl.multiple_of(step * block, block)
    allowed = allowed_pairs(length, block, start, prefix_ref[0])
    query = x_ref[pl.ds(start, block), :width]
    heads = width // HEAD_DIM

    @pl.when(step == 0)
    def _():
        key_acc[...] = jnp.zeros_like(key_acc)
        value_acc[...] = jnp.zeros_like(value_acc)

    parts = []
    for h in range(heads):
        own = query[:, h * HEAD_DIM : (h + 1) * HEAD_DIM] * HEAD_DIM ** (-0.5)
        grad = grad_ref[:, h * HEAD_DIM : (h + 1) * HEAD_DIM]
        keys, values, weights, total = head_probs(x_ref, own, allowed, width, h)
        probs = weights * (1.0 / total)
        prob_grad = contract_cols(values, grad)
        inner = jnp.sum(probs * prob_grad, 0, keepdims=True)
        score_grad = (probs * (prob_grad - inner)).astype(jnp.bfloat16)
        value_acc[h] += jnp.dot(
            probs.astype(jnp.bfloat16), grad, preferred_element_type=jnp.float32
        )
        key_acc[h] += jnp.dot(score_grad, own, preferred_element_type=jnp.float32)
        parts.append(contract_rows(keys, score_grad) * HEAD_DIM ** (-0.5))
    out_ref[pl.ds(start, block), :width] = jnp.concatenate(parts, 0).T.astype(out_ref.dtype)

    @pl.when(step == pl.num_programs(0) - 1)
    def _():
        out_ref[:, width : 2 * width] = jnp.concatenate(
            [key_acc[h] for h in range(heads)], 1
        ).astype(out_ref.dtype)
        out_ref[:, 2 * width :] = jnp.concatenate(
            [value_acc[h] for h in range(heads)], 1
        ).astype(out_ref.dtype)


def attend_back(whole, grads, prefix, block):
    length, cols = whole.shape
    width = cols // 3
    heads = width // HEAD_DIM
    return pl.pallas_call(
        attend_back_kernel,
        out_shape=jax.ShapeDtypeStruct((length, cols), whole.dtype),
        grid=(length // block,),
        in_specs=[
            pl.BlockSpec(memory_space=pltpu.SMEM),
            pl.BlockSpec((length, cols), lambda i: (0, 0)),
            pl.BlockSpec((block, width), lambda i: (i, 0)),
        ],
        out_specs=pl.BlockSpec((length, cols), lambda i: (0, 0)),
        scratch_shapes=[
            pltpu.VMEM((heads, length, HEAD_DIM), jnp.float32),
            pltpu.VMEM((heads, length, HEAD_DIM), jnp.float32),
        ],
        cost_estimate=attend_cost(length, cols, 10),
        name="attend_back",
    )(prefix, whole, grads)


def after(value, *others):
    return lax.optimization_barrier((value,) + others)[0]


def flip(values, bit):
    count = lax.axis_size("dp")
    return lax.ppermute(values, "dp", [(i, i ^ bit) for i in range(count)])


def near_groups():
    count = lax.axis_size("dp")
    return [[i, i ^ 1] for i in range(count) if not i & 1]


def gather_near(shard):
    return lax.all_gather(shard, "dp", axis=0, axis_index_groups=near_groups())


def scatter_near(parts):
    return lax.psum_scatter(parts, "dp", scatter_dimension=0, axis_index_groups=near_groups())


def both_rows(own):
    return jnp.concatenate([own, flip(own, 2)], 0)


def sum_pair(partial_sums):
    size = partial_sums.shape[0] // 2
    received = flip(partial_sums, 2)
    return partial_sums.astype(jnp.float32) + jnp.concatenate(
        [received[size:], received[:size]], 0
    ).astype(jnp.float32)


def sum_own(partial_sums):
    size = partial_sums.shape[0] // 2
    received = flip(partial_sums[size:], 2)
    return partial_sums[:size].astype(jnp.float32) + received.astype(jnp.float32)


def shards(
    tokens,
    cotangent,
    routes,
    prefix,
    qkv_weight,
    mix_weight,
    up_weight,
    down_weight,
    dense_gain,
    expert_up,
    expert_down,
    expert_gain,
    centroids,
):
    f32, low = jnp.float32, jnp.bfloat16
    micro_count, _, rows_dev, width = tokens.shape
    dp_count = lax.axis_size("dp")
    experts = lax.axis_size("expert")
    capacity = max(2, 5 * rows_dev // (4 * experts))
    length = rows_dev * dp_count
    mine = width // dp_count
    block = min(256, length)
    micros = range(micro_count)
    slot_ids = jnp.arange(experts * capacity, dtype=jnp.int32)
    expert_ids = jnp.arange(experts, dtype=jnp.int32)
    up_ex, down_ex, centroid = (expert_up[0], expert_down[0], centroids[0])
    gain_ex = expert_gain[0].astype(f32)

    places, grad_rows = ([], [])
    for micro in micros:
        route = routes[micro, 0, :, 0]
        onehot = (route[:, None] == expert_ids[None, :]).astype(jnp.int32)
        rank = jnp.sum((jnp.cumsum(onehot, 0) - 1) * onehot, 1)
        slot = route * capacity + rank
        place = (slot[None, :] == slot_ids[:, None]).astype(low)
        places.append(place)
        grad_sent = jnp.dot(
            place, cotangent[micro, 0].astype(low), preferred_element_type=f32
        ).astype(low)
        grad_rows.append(both_rows(swap_experts(grad_sent)))

    order_a, order_b = bit_orders()
    rows_qkv = qkv_weight.shape[0]
    by_dest = (
        qkv_weight.reshape(rows_qkv, 3, dp_count, mine)
        .transpose(0, 2, 1, 3)
        .reshape(rows_qkv, 3 * width)
    )
    half = 3 * width // 2
    gain_cols = jnp.pad(dense_gain.T, ((0, 0), (0, 126)))
    first = turn_gather(jnp.concatenate([by_dest, gain_cols], 1))
    part_a = spread(first[:, :, :half], order_a)
    part_b = spread(first[:, :, half:], order_b)
    qkv_pieces = dict(part_b)
    full_qkv = assemble(
        [(mask, jnp.concatenate([piece, qkv_pieces[mask][:, :, :half]], 2)) for mask, piece in part_a]
    )
    full_gain = assemble([(mask, piece[:, :, half:]) for mask, piece in part_b])
    gains = full_gain[:, :2].T.astype(f32)
    full_mix = assemble(spread(turn_gather(mix_weight), order_a))
    full_up = assemble(spread(gather_dp(up_weight), order_a))
    full_down = assemble(spread(gather_dp(down_weight), order_b))

    up_both, down_both = ([], [])
    for layer in range(2):
        up_near = gather_near(after(up_ex[layer], first))
        up_both.append(jnp.concatenate([up_near[0], up_near[1]], 1))
        down_both.append(gather_near(after(down_ex[layer], first)).reshape(-1, width))

    dense = []
    slots_in = []
    for micro in micros:
        source = tokens[micro, 0]
        if micro > 0:
            source = after(source, slots_in[micro - 1])
        inputs = source.astype(f32)
        normed = layer_norm(inputs, gains[0]).astype(low)
        qkv = jnp.dot(normed, full_qkv, preferred_element_type=f32).astype(low)
        blocks = qkv.reshape(rows_dev, dp_count, 3 * mine).transpose(1, 0, 2)
        whole = swap_heads(blocks).reshape(length, 3 * mine)
        mixed = attend(whole, prefix[micro], block).reshape(dp_count, rows_dev, mine)
        mixed = swap_heads(mixed).transpose(1, 0, 2).reshape(rows_dev, width)
        attn = jnp.dot(mixed, full_mix, preferred_element_type=f32)
        resid = inputs + attn
        normed2 = layer_norm(resid, gains[1]).astype(low)
        pre = jnp.dot(normed2, full_up, preferred_element_type=f32)
        hidden = gelu(pre).astype(low)
        ffn = jnp.dot(hidden, full_down, preferred_element_type=f32)
        dense_out = resid + ffn
        sent = jnp.dot(places[micro], dense_out.astype(low), preferred_element_type=f32).astype(low)
        dense.append((inputs, normed, whole, mixed, attn, resid, ffn, normed2, pre, hidden, dense_out))
        slots_in.append(swap_experts(sent))

    slot_count = experts * capacity
    gain_one = jnp.zeros((width,), f32)
    first_stage = []
    for micro in micros:
        rows = both_rows(slots_in[micro])
        if micro > 0:
            rows = after(rows, first_stage[micro - 1][-1])
        sig = jax.nn.sigmoid(jnp.dot(rows, centroid, preferred_element_type=f32))[:, None]
        state0 = rows.astype(f32)
        z0 = layer_norm(state0, gain_ex[0]).astype(low)
        pre0 = jnp.dot(z0, up_both[0], preferred_element_type=f32)
        h0 = gelu(pre0).astype(low)
        out0 = jnp.dot(h0, down_both[0], preferred_element_type=f32).astype(low)
        first_stage.append((rows, sig, z0, pre0, h0, out0))
    second_stage = []
    for micro in micros:
        rows, sig = first_stage[micro][:2]
        total = sum_pair(first_stage[micro][-1])
        if micro > 0:
            total = after(total, second_stage[micro - 1][-1])
        state1 = rows.astype(f32) + total
        z1 = layer_norm(state1, gain_ex[1]).astype(low)
        pre1 = jnp.dot(z1, up_both[1], preferred_element_type=f32)
        h1 = gelu(pre1).astype(low)
        out1 = jnp.dot(h1, down_both[1], preferred_element_type=f32).astype(low)
        incoming = grad_rows[micro].astype(f32)
        grad2 = incoming * sig
        grad_y = grad2.astype(low)
        pre_grad = gelu_back(pre1, contract_cols(grad_y, down_both[1])).astype(low)
        normed_part = contract_cols(pre_grad, up_both[1]).astype(low)
        second_stage.append((state1, out1, incoming, grad2, z1, h1, grad_y, pre_grad, normed_part))
    hidden_dev = up_ex.shape[2]
    hidden_halves = (slice(0, hidden_dev), slice(hidden_dev, 2 * hidden_dev))

    def grad_halves(lefts, rights, split_left):
        left, right = (jnp.concatenate(parts, 0) for parts in (lefts, rights))
        return jnp.stack(
            [
                contract_rows(left[:, half] if split_left else left, right if split_left else right[:, half])
                for half in hidden_halves
            ]
        ).astype(low)

    up_grads, down_grads = ([None, None], [None, None])
    by_stage = list(zip(*second_stage))
    down_grads[1] = grad_halves(by_stage[5], by_stage[6], True)
    up_grads[1] = grad_halves(by_stage[4], by_stage[7], False)
    third_stage = []
    for micro in micros:
        rows, sig, z0, pre0, h0, _ = first_stage[micro]
        state1, out1, incoming, grad2 = second_stage[micro][:4]
        total = sum_pair(second_stage[micro][-1])
        if micro > 0:
            total = after(total, third_stage[micro - 1][-1], up_grads[1], down_grads[1])
        state_grad, gain_grad = norm_back(state1, gain_ex[1], total)
        gain_one = gain_one + gain_grad
        grad1 = grad2 + state_grad
        grad_y = grad1.astype(low)
        pre_grad = gelu_back(pre0, contract_cols(grad_y, down_both[0])).astype(low)
        normed_part = contract_cols(pre_grad, up_both[0]).astype(low)
        third_stage.append((grad1, grad_y, pre_grad, normed_part))
    by_first, by_third = (list(zip(*first_stage)), list(zip(*third_stage)))
    down_grads[0] = grad_halves(by_first[4], by_third[1], True)
    up_grads[0] = grad_halves(by_first[2], by_third[2], False)
    down_sum, up_sum = ([None, None], [None, None])
    for layer in (1, 0):
        down_sum[layer] = scatter_near(down_grads[layer]).astype(f32)
        up_sum[layer] = scatter_near(up_grads[layer]).astype(f32)
    own_grads = []
    branches = []
    for micro in micros:
        rows, sig = first_stage[micro][:2]
        state1, out1, incoming = second_stage[micro][:3]
        grad1, normed_part = (third_stage[micro][i] for i in (0, 3))
        normed_grad = sum_own(normed_part)
        own_rows = rows[:slot_count].astype(f32)
        state_grad, gain_grad = norm_back(own_rows, gain_ex[0], normed_grad)
        own_sig = sig[:slot_count]
        state2 = state1[:slot_count] + sum_own(out1)
        branches.append((own_sig * state2).astype(low))
        score_grad = jnp.sum(incoming[:slot_count] * state2, 1, keepdims=True)
        score_grad = score_grad * own_sig * (1.0 - own_sig)
        row_grad = grad1[:slot_count] + state_grad + score_grad * centroid.astype(f32)
        cent_grad = jnp.sum(score_grad * own_rows, 0)
        own_grads.append((row_grad.astype(low), gain_grad, cent_grad))

    gain_acc = jnp.zeros((2, width), f32)
    input_grads = []
    kept = []
    kept_dense = []
    order_c, order_d = (order_a[::-1], order_b[::-1])
    for micro in micros:
        inputs, normed, whole, mixed, attn, resid, ffn, normed2, pre, hidden, _ = dense[micro]
        grad_back = swap_experts(own_grads[micro][0])
        after_grad = cotangent[micro, 0] + contract_rows(places[micro], grad_back)
        ffn_low = after_grad.astype(low)
        hidden_grad = contract_cols(ffn_low, full_down)
        pre_grad = gelu_back(pre, hidden_grad).astype(low)
        normed2_grad = contract_cols(pre_grad, full_up)
        resid_part, gain2_grad = norm_back(resid, gains[1], normed2_grad)
        resid_grad = after_grad + resid_part
        attn_low = resid_grad.astype(low)
        mixed_grad = contract_cols(attn_low, full_mix).astype(low)
        mixed_grad = mixed_grad.reshape(rows_dev, dp_count, mine).transpose(1, 0, 2)
        mixed_grad = swap_heads(mixed_grad).reshape(length, mine)
        kept_dense.append((normed2, pre_grad, hidden, ffn_low))
        if micro == 0:
            mixed_grad = after(mixed_grad, up_grads[0], down_grads[0], down_sum[1])
        if micro == micro_count - 1:
            joined = [jnp.concatenate(parts, 0) for parts in zip(*kept_dense)]
            down_start = scatter_start(contract_rows(joined[2], joined[3]).astype(low), order_c)
            up_low = contract_rows(joined[0], joined[1]).astype(low)
            mixed_grad = after(mixed_grad, down_start[0], up_low, up_sum[1])
        whole_grad = attend_back(whole, mixed_grad, prefix[micro], block)
        qkv_grad = swap_heads(whole_grad.reshape(dp_count, rows_dev, 3 * mine))
        qkv_grad = qkv_grad.transpose(1, 0, 2).reshape(rows_dev, 3 * width)
        if micro == micro_count - 1:
            qkv_grad = after(qkv_grad, down_sum[0])
        normed_grad = contract_cols(qkv_grad, full_qkv)
        input_part, gain1_grad = norm_back(inputs, gains[0], normed_grad)
        input_grads.append(resid_grad + input_part)
        gain_acc = gain_acc + jnp.stack([gain1_grad, gain2_grad])
        kept.append((normed, qkv_grad, mixed, attn_low))
    joined = [jnp.concatenate(parts, 0) for parts in zip(*kept)]
    down_out = scatter_end(down_start)
    up_out = scatter_rows(up_low, order_d)
    mix_out = scatter_rows(contract_rows(joined[2], joined[3]).astype(low), order_d)
    qkv_low = contract_rows(joined[0], joined[1]).astype(low)
    qkv_out = jnp.concatenate(
        [scatter_rows(qkv_low[:, :half], order_c), scatter_rows(qkv_low[:, half:], order_d)], 1
    )
    qkv_out = (
        qkv_out.reshape(rows_qkv, dp_count, 3, mine)
        .transpose(0, 2, 1, 3)
        .reshape(rows_qkv, 3 * width)
    )

    output_list = []
    stat_list = []
    for micro in micros:
        attn, ffn, dense_out = (dense[micro][i] for i in (4, 6, 10))
        returned = swap_experts(branches[micro])
        branch = contract_rows(places[micro], returned)
        final = dense_out + branch
        output_list.append(final.astype(low))
        stat_list.append(jnp.stack([jnp.sum(v * v) for v in (final, attn, ffn, branch)]))

    small = jnp.concatenate(
        [
            jnp.stack(stat_list, 1).reshape(-1),
            sum(part[1] for part in own_grads),
            sum(part[2] for part in own_grads),
            0.5 * gain_one,
        ]
    )
    small = sum_small(small)
    stats = 4 * micro_count
    branch_rms = jnp.sqrt(small[:stats] / (length * width)).reshape(4, micro_count, 1)
    ex_gain = jnp.stack([small[stats : stats + width], small[stats + 2 * width :]])
    gain_sum = sum_small(gain_acc)
    for bit in order_a:
        gain_sum = gain_sum + swap(gain_sum, bit)
    device = lax.axis_index("dp") * experts + lax.axis_index("expert")
    gain_out = lax.dynamic_index_in_dim(
        gain_sum.reshape(2, dp_count * experts, -1), device, 1, keepdims=False
    )
    return (
        jnp.stack(output_list)[:, None],
        jnp.stack(input_grads)[:, None],
        qkv_out,
        mix_out,
        up_out,
        down_out,
        gain_out,
        jnp.stack(up_sum)[None],
        jnp.stack(down_sum)[None],
        ex_gain[None],
        small[None, stats + width : stats + 2 * width],
        branch_rms,
    )


def solution(mesh):
    return jax.shard_map(
        shards,
        mesh=mesh,
        in_specs=(
            P(None, "expert", "dp", None),
            P(None, "expert", "dp", None),
            P(None, "expert", "dp", None),
            P(None, "expert"),
            P(("dp", "expert"), None),
            P(("dp", "expert"), None),
            P(("dp", "expert"), None),
            P(("dp", "expert"), None),
            P(None, ("dp", "expert")),
            P("expert", None, None, "dp"),
            P("expert", None, "dp", None),
            P("expert", None, None),
            P("expert", None),
        ),
        out_specs=(
            P(None, "expert", "dp", None),
            P(None, "expert", "dp", None),
            P(("dp", "expert"), None),
            P(("dp", "expert"), None),
            P(("dp", "expert"), None),
            P(("dp", "expert"), None),
            P(None, ("dp", "expert")),
            P("expert", None, None, "dp"),
            P("expert", None, "dp", None),
            P("expert", None, None),
            P("expert", None),
            P(None, None, "expert"),
        ),
        check_vma=False,
    )
```

```python
import functools

import jax
import jax.numpy as jnp
from jax import lax
from jax.experimental import pallas as pl
from jax.experimental.pallas import tpu as pltpu
from jax.sharding import PartitionSpec as P

HEAD_DIM = 64


eps = 1e-05


def layer_norm(values, gain):
    centred = values - jnp.mean(values, -1, keepdims=True)
    spread = jnp.mean(centred * centred, -1, keepdims=True)
    return centred * lax.rsqrt(spread + eps) * gain


def norm_back(values, gain, grads):
    _, pullback = jax.vjp(layer_norm, values, gain)
    return pullback(grads)


def gelu(values):
    return jax.nn.gelu(values, approximate=True)


def gelu_back(values, grads):
    _, pullback = jax.vjp(gelu, values)
    return pullback(grads)[0]


def contract_rows(left, right):
    return lax.dot_general(
        left, right, (((0,), (0,)), ((), ())), preferred_element_type=jnp.float32
    )


def contract_cols(left, right):
    return lax.dot_general(
        left, right, (((1,), (1,)), ((), ())), preferred_element_type=jnp.float32
    )


def swap(values, bit):
    count = lax.axis_size("expert")
    return lax.ppermute(values, "expert", [(i, i ^ bit) for i in range(count)])


def turn(values, shift):
    count = lax.axis_size("dp")
    return lax.ppermute(values, "dp", [(i, (i + shift) % count) for i in range(count)])


def sum_small(values):
    total = values
    for shift in range(1, lax.axis_size("dp")):
        total = total + turn(values, shift)
    return total


def bit_orders():
    count = lax.axis_size("expert")
    bits = [1 << i for i in range(count.bit_length() - 1)]
    upper = bits[1:]
    half = len(upper) // 2
    return upper[half:] + upper[:half] + bits[:1], upper[:half] + upper[half:] + bits[:1]


def assemble_kernel(masks, *refs):
    count = len(masks)
    pieces, full, held, in_sems, out_sems = (
        refs[:count],
        refs[count],
        refs[count + 1],
        refs[count + 2],
        refs[count + 3],
    )
    own = lax.axis_index("expert")
    loads = [pltpu.make_async_copy(pieces[i], held.at[i], in_sems.at[i]) for i in range(count)]
    stores = [
        pltpu.make_async_copy(
            held.at[i], full.at[:, jnp.bitwise_xor(own, mask)], out_sems.at[i]
        )
        for i, mask in enumerate(masks)
    ]
    for load in loads:
        load.start()
    for load, store in zip(loads, stores):
        load.wait()
        store.start()
    for store in stores:
        store.wait()


def assemble(pieces):
    masks = [mask for mask, _ in pieces]
    arrays = [piece for _, piece in pieces]
    dp_count, rows, cols = arrays[0].shape
    full = pl.pallas_call(
        functools.partial(assemble_kernel, masks),
        out_shape=jax.ShapeDtypeStruct((dp_count, len(masks), rows, cols), arrays[0].dtype),
        in_specs=[pl.BlockSpec(memory_space=pl.ANY)] * len(masks),
        out_specs=pl.BlockSpec(memory_space=pl.ANY),
        scratch_shapes=[
            pltpu.VMEM((len(masks), dp_count, rows, cols), arrays[0].dtype),
            pltpu.SemaphoreType.DMA((len(masks),)),
            pltpu.SemaphoreType.DMA((len(masks),)),
        ],
        name="assemble",
    )(*arrays)
    return full.reshape(dp_count * len(masks) * rows, cols)


def spread(piece, order):
    pieces = [(0, piece)]
    for bit in order:
        pieces = pieces + [(mask ^ bit, swap(part, bit)) for mask, part in pieces]
    return pieces


def gather_dp(shard):
    return lax.all_gather(shard, "dp", axis=0)


def turn_gather(shard):
    count = lax.axis_size("dp")
    own = lax.axis_index("dp")
    full = jnp.zeros((count,) + shard.shape, shard.dtype)
    for shift in range(count):
        part = shard if shift == 0 else turn(shard, shift)
        full = lax.dynamic_update_slice_in_dim(full, part[None], (own - shift) % count, 0)
    return full


def scatter_start(total, order):
    count = lax.axis_size("expert")
    dp_count = lax.axis_size("dp")
    rows = total.shape[0] // (count * dp_count)
    bits = sorted(order)
    current = total.reshape((dp_count,) + (2,) * len(bits) + (rows, total.shape[1]))
    left = sorted(bits, reverse=True)
    return scatter_bits(current, order[:1], left), order[1:], left


def scatter_bits(current, order, left):
    own = lax.axis_index("expert")
    for bit in order:
        axis = 1 + left.index(bit)
        mine = (own // bit) % 2
        send = lax.dynamic_index_in_dim(current, 1 - mine, axis, keepdims=False)
        keep = lax.dynamic_index_in_dim(current, mine, axis, keepdims=False)
        received = swap(send, bit)
        current = (keep.astype(jnp.float32) + received.astype(jnp.float32)).astype(jnp.bfloat16)
        left.remove(bit)
    return current


def scatter_end(started):
    current, order, left = started
    current = scatter_bits(current, order, left)
    return lax.psum_scatter(
        current.reshape(-1, current.shape[-1]), "dp", scatter_dimension=0, tiled=True
    ).astype(jnp.float32)


def scatter_rows(total, order):
    return scatter_end(scatter_start(total, order))


def swap_heads(blocks):
    return lax.all_to_all(blocks, "dp", split_axis=0, concat_axis=0, tiled=True)


def swap_experts(slots):
    count = lax.axis_size("expert")
    blocks = slots.reshape(count, -1, slots.shape[1])
    return lax.all_to_all(blocks, "expert", split_axis=0, concat_axis=0, tiled=True).reshape(
        slots.shape
    )


def head_probs(x_ref, query, allowed, width, h):
    keys = x_ref[:, width + h * HEAD_DIM : width + (h + 1) * HEAD_DIM]
    values = x_ref[:, 2 * width + h * HEAD_DIM : 2 * width + (h + 1) * HEAD_DIM]
    scores = jnp.where(allowed, contract_cols(keys, query), -1e30)
    top = jnp.max(scores, 0, keepdims=True)
    weights = jnp.exp(scores - top)
    return keys, values, weights, jnp.sum(weights, 0, keepdims=True)


def allowed_pairs(length, block, start, prefix):
    key_pos = lax.broadcasted_iota(jnp.int32, (length, block), 0)
    query_pos = start + lax.broadcasted_iota(jnp.int32, (length, block), 1)
    return (key_pos <= query_pos) | (key_pos < prefix)


def attend_kernel(prefix_ref, x_ref, out_ref):
    block, width = out_ref.shape
    length = x_ref.shape[0]
    start = pl.multiple_of(pl.program_id(0) * block, block)
    allowed = allowed_pairs(length, block, start, prefix_ref[0])
    query = x_ref[pl.ds(start, block), :width]
    parts = []
    for h in range(width // HEAD_DIM):
        own = query[:, h * HEAD_DIM : (h + 1) * HEAD_DIM] * HEAD_DIM ** (-0.5)
        _, values, weights, total = head_probs(x_ref, own, allowed, width, h)
        parts.append(contract_rows(values, weights.astype(jnp.bfloat16)) * (1.0 / total))
    out_ref[...] = jnp.concatenate(parts, 0).T.astype(out_ref.dtype)


def attend_cost(length, cols, products):
    return pl.CostEstimate(
        flops=products * length * length * cols // 3,
        transcendentals=length * length * cols // (3 * HEAD_DIM),
        bytes_accessed=products * length * cols,
    )


def attend(whole, prefix, block):
    length, cols = whole.shape
    width = cols // 3
    return pl.pallas_call(
        attend_kernel,
        out_shape=jax.ShapeDtypeStruct((length, width), whole.dtype),
        grid=(length // block,),
        in_specs=[
            pl.BlockSpec(memory_space=pltpu.SMEM),
            pl.BlockSpec((length, cols), lambda i: (0, 0)),
        ],
        out_specs=pl.BlockSpec((block, width), lambda i: (i, 0)),
        cost_estimate=attend_cost(length, cols, 4),
        name="attend",
    )(prefix, whole)


def attend_back_kernel(prefix_ref, x_ref, grad_ref, out_ref, key_acc, value_acc):
    block, width = grad_ref.shape
    length = x_ref.shape[0]
    step = pl.program_id(0)
    start = pl.multiple_of(step * block, block)
    allowed = allowed_pairs(length, block, start, prefix_ref[0])
    query = x_ref[pl.ds(start, block), :width]
    heads = width // HEAD_DIM

    @pl.when(step == 0)
    def _():
        key_acc[...] = jnp.zeros_like(key_acc)
        value_acc[...] = jnp.zeros_like(value_acc)

    parts = []
    for h in range(heads):
        own = query[:, h * HEAD_DIM : (h + 1) * HEAD_DIM] * HEAD_DIM ** (-0.5)
        grad = grad_ref[:, h * HEAD_DIM : (h + 1) * HEAD_DIM]
        keys, values, weights, total = head_probs(x_ref, own, allowed, width, h)
        probs = weights * (1.0 / total)
        prob_grad = contract_cols(values, grad)
        inner = jnp.sum(probs * prob_grad, 0, keepdims=True)
        score_grad = (probs * (prob_grad - inner)).astype(jnp.bfloat16)
        value_acc[h] += jnp.dot(
            probs.astype(jnp.bfloat16), grad, preferred_element_type=jnp.float32
        )
        key_acc[h] += jnp.dot(score_grad, own, preferred_element_type=jnp.float32)
        parts.append(contract_rows(keys, score_grad) * HEAD_DIM ** (-0.5))
    out_ref[pl.ds(start, block), :width] = jnp.concatenate(parts, 0).T.astype(out_ref.dtype)

    @pl.when(step == pl.num_programs(0) - 1)
    def _():
        out_ref[:, width : 2 * width] = jnp.concatenate(
            [key_acc[h] for h in range(heads)], 1
        ).astype(out_ref.dtype)
        out_ref[:, 2 * width :] = jnp.concatenate(
            [value_acc[h] for h in range(heads)], 1
        ).astype(out_ref.dtype)


def attend_back(whole, grads, prefix, block):
    length, cols = whole.shape
    width = cols // 3
    heads = width // HEAD_DIM
    return pl.pallas_call(
        attend_back_kernel,
        out_shape=jax.ShapeDtypeStruct((length, cols), whole.dtype),
        grid=(length // block,),
        in_specs=[
            pl.BlockSpec(memory_space=pltpu.SMEM),
            pl.BlockSpec((length, cols), lambda i: (0, 0)),
            pl.BlockSpec((block, width), lambda i: (i, 0)),
        ],
        out_specs=pl.BlockSpec((length, cols), lambda i: (0, 0)),
        scratch_shapes=[
            pltpu.VMEM((heads, length, HEAD_DIM), jnp.float32),
            pltpu.VMEM((heads, length, HEAD_DIM), jnp.float32),
        ],
        cost_estimate=attend_cost(length, cols, 10),
        name="attend_back",
    )(prefix, whole, grads)


def after(value, *others):
    return lax.optimization_barrier((value,) + others)[0]


def flip(values, bit):
    count = lax.axis_size("dp")
    return lax.ppermute(values, "dp", [(i, i ^ bit) for i in range(count)])


def near_groups():
    count = lax.axis_size("dp")
    return [[i, i ^ 1] for i in range(count) if not i & 1]


def gather_near(shard):
    return lax.all_gather(shard, "dp", axis=0, axis_index_groups=near_groups())


def scatter_near(parts):
    return lax.psum_scatter(parts, "dp", scatter_dimension=0, axis_index_groups=near_groups())


def both_rows(own):
    return jnp.concatenate([own, flip(own, 2)], 0)


def sum_pair(partial_sums):
    size = partial_sums.shape[0] // 2
    received = flip(partial_sums, 2)
    return partial_sums.astype(jnp.float32) + jnp.concatenate(
        [received[size:], received[:size]], 0
    ).astype(jnp.float32)


def sum_own(partial_sums):
    size = partial_sums.shape[0] // 2
    received = flip(partial_sums[size:], 2)
    return partial_sums[:size].astype(jnp.float32) + received.astype(jnp.float32)


def shards(
    tokens,
    cotangent,
    routes,
    prefix,
    qkv_weight,
    mix_weight,
    up_weight,
    down_weight,
    dense_gain,
    expert_up,
    expert_down,
    expert_gain,
    centroids,
):
    f32, low = jnp.float32, jnp.bfloat16
    micro_count, _, rows_dev, width = tokens.shape
    dp_count = lax.axis_size("dp")
    experts = lax.axis_size("expert")
    capacity = max(2, 5 * rows_dev // (4 * experts))
    length = rows_dev * dp_count
    mine = width // dp_count
    block = min(256, length)
    micros = range(micro_count)
    slot_ids = jnp.arange(experts * capacity, dtype=jnp.int32)
    expert_ids = jnp.arange(experts, dtype=jnp.int32)
    up_ex, down_ex, centroid = (expert_up[0], expert_down[0], centroids[0])
    gain_ex = expert_gain[0].astype(f32)

    places, grad_rows = ([], [])
    for micro in micros:
        route = routes[micro, 0, :, 0]
        onehot = (route[:, None] == expert_ids[None, :]).astype(jnp.int32)
        rank = jnp.sum((jnp.cumsum(onehot, 0) - 1) * onehot, 1)
        slot = route * capacity + rank
        place = (slot[None, :] == slot_ids[:, None]).astype(low)
        places.append(place)
        grad_sent = jnp.dot(
            place, cotangent[micro, 0].astype(low), preferred_element_type=f32
        ).astype(low)
        grad_rows.append(both_rows(swap_experts(grad_sent)))

    order_a, order_b = bit_orders()
    rows_qkv = qkv_weight.shape[0]
    by_dest = (
        qkv_weight.reshape(rows_qkv, 3, dp_count, mine)
        .transpose(0, 2, 1, 3)
        .reshape(rows_qkv, 3 * width)
    )
    half = 3 * width // 2
    gain_cols = jnp.pad(dense_gain.T, ((0, 0), (0, 126)))
    first = turn_gather(jnp.concatenate([by_dest, gain_cols], 1))
    part_a = spread(first[:, :, :half], order_a)
    part_b = spread(first[:, :, half:], order_b)
    qkv_pieces = dict(part_b)
    full_qkv = assemble(
        [(mask, jnp.concatenate([piece, qkv_pieces[mask][:, :, :half]], 2)) for mask, piece in part_a]
    )
    mix_dp = turn_gather(mix_weight)
    full_qkv = after(full_qkv, mix_dp)
    full_gain = assemble([(mask, piece[:, :, half:]) for mask, piece in part_b])
    gains = full_gain[:, :2].T.astype(f32)
    full_mix = assemble(spread(mix_dp, order_a))
    up_pieces = spread(gather_dp(up_weight), order_a)
    down_pieces = spread(gather_dp(down_weight), order_b)
    full_up, full_down = (assemble(up_pieces), assemble(down_pieces))
    hops = [
        [piece for pieces in (up_pieces, down_pieces) for _, piece in pieces[start : 2 * start]]
        for start in (1, 2)
    ]

    up_both, down_both = ([], [])
    for layer in range(2):
        up_near = gather_near(after(up_ex[layer], first))
        up_both.append(jnp.concatenate([up_near[0], up_near[1]], 1))
        down_both.append(gather_near(after(down_ex[layer], first)).reshape(-1, width))

    dense = []
    slots_in = []
    sends, mixes = ([], [])
    for micro in micros:
        source = tokens[micro, 0]
        if micro > 0:
            source = after(source, slots_in[micro - 1])
        inputs = source.astype(f32)
        normed = layer_norm(inputs, gains[0]).astype(low)
        qkv = jnp.dot(normed, full_qkv, preferred_element_type=f32).astype(low)
        blocks = qkv.reshape(rows_dev, dp_count, 3 * mine).transpose(1, 0, 2)
        whole = swap_heads(blocks).reshape(length, 3 * mine)
        if micro == 0:
            whole = after(whole, *hops[0])
        mixed = attend(whole, prefix[micro], block).reshape(dp_count, rows_dev, mine)
        mixed = swap_heads(mixed)
        mixes.append(mixed)
        if micro == 0:
            mixed = after(mixed, *hops[1])
        mixed = mixed.transpose(1, 0, 2).reshape(rows_dev, width)
        attn = jnp.dot(mixed, full_mix, preferred_element_type=f32)
        resid = inputs + attn
        normed2 = layer_norm(resid, gains[1]).astype(low)
        pre = jnp.dot(normed2, full_up, preferred_element_type=f32)
        hidden = gelu(pre).astype(low)
        ffn = jnp.dot(hidden, full_down, preferred_element_type=f32)
        dense_out = resid + ffn
        sent = jnp.dot(places[micro], dense_out.astype(low), preferred_element_type=f32).astype(low)
        dense.append((inputs, normed, whole, mixed, attn, resid, ffn, normed2, pre, hidden, dense_out))
        sends.append(sent)
        slots_in.append(swap_experts(sent))

    slot_count = experts * capacity
    first_stage = []
    for micro in micros:
        rows = both_rows(slots_in[micro])
        if micro > 0:
            rows = after(rows, first_stage[micro - 1][-1])
        sig = jax.nn.sigmoid(jnp.dot(rows, centroid, preferred_element_type=f32))[:, None]
        state0 = rows.astype(f32)
        z0 = layer_norm(state0, gain_ex[0]).astype(low)
        pre0 = jnp.dot(z0, up_both[0], preferred_element_type=f32)
        h0 = gelu(pre0).astype(low)
        out0 = jnp.dot(h0, down_both[0], preferred_element_type=f32).astype(low)
        first_stage.append((rows, sig, z0, pre0, h0, out0))
    second_stage = []

    def run_second(micro, *others):
        rows, sig = first_stage[micro][:2]
        total = sum_pair(first_stage[micro][-1])
        total = after(total, *others)
        state1 = rows.astype(f32) + total
        z1 = layer_norm(state1, gain_ex[1]).astype(low)
        pre1 = jnp.dot(z1, up_both[1], preferred_element_type=f32)
        h1 = gelu(pre1).astype(low)
        out1 = jnp.dot(h1, down_both[1], preferred_element_type=f32).astype(low)
        incoming = grad_rows[micro].astype(f32)
        grad2 = incoming * sig
        grad_y = grad2.astype(low)
        pre_grad = gelu_back(pre1, contract_cols(grad_y, down_both[1])).astype(low)
        normed_part = contract_cols(pre_grad, up_both[1]).astype(low)
        second_stage.append((state1, out1, incoming, grad2, z1, h1, grad_y, pre_grad, normed_part))

    hidden_dev = up_ex.shape[2]
    hidden_halves = (slice(0, hidden_dev), slice(hidden_dev, 2 * hidden_dev))

    def grad_halves(lefts, rights, split_left):
        left, right = (jnp.concatenate(parts, 0) for parts in (lefts, rights))
        return jnp.stack(
            [
                contract_rows(left[:, half] if split_left else left, right if split_left else right[:, half])
                for half in hidden_halves
            ]
        ).astype(low)

    gain_ones = []
    third_stage = []

    def run_third(micro, *others):
        rows, sig, z0, pre0, h0, _ = first_stage[micro]
        state1, out1, incoming, grad2 = second_stage[micro][:4]
        total = sum_pair(second_stage[micro][-1])
        total = after(total, *others)
        state_grad, gain_grad = norm_back(state1, gain_ex[1], total)
        grad1 = grad2 + state_grad
        grad_y = grad1.astype(low)
        pre_grad = gelu_back(pre0, contract_cols(grad_y, down_both[0])).astype(low)
        normed_part = contract_cols(pre_grad, up_both[0]).astype(low)
        third_stage.append((grad1, grad_y, pre_grad, normed_part))
        gain_ones.append(gain_grad)
    own_grads = []
    branches = []

    def run_own(micro, *others):
        rows, sig = first_stage[micro][:2]
        state1, out1, incoming = second_stage[micro][:3]
        grad1, normed_part = (third_stage[micro][i] for i in (0, 3))
        normed_grad = after(sum_own(normed_part), *others)
        own_rows = rows[:slot_count].astype(f32)
        state_grad, gain_grad = norm_back(own_rows, gain_ex[0], normed_grad)
        own_sig = sig[:slot_count]
        state2 = state1[:slot_count] + sum_own(out1)
        branches.append((own_sig * state2).astype(low))
        score_grad = jnp.sum(incoming[:slot_count] * state2, 1, keepdims=True)
        score_grad = score_grad * own_sig * (1.0 - own_sig)
        row_grad = grad1[:slot_count] + state_grad + score_grad * centroid.astype(f32)
        cent_grad = jnp.sum(score_grad * own_rows, 0)
        own_grads.append((row_grad.astype(low), gain_grad, cent_grad))

    gain_sums, resid_grads, late = ([], [], [])
    input_grads = []
    kept = []
    kept_dense = []
    order_c, order_d = (order_a[::-1], order_b[::-1])
    whole_grads = []

    def run_ffn_back(micro):
        inputs, normed, whole, mixed, attn, resid, ffn, normed2, pre, hidden, _ = dense[micro]
        grad_back = swap_experts(own_grads[micro][0])
        after_grad = cotangent[micro, 0] + contract_rows(places[micro], grad_back)
        ffn_low = after_grad.astype(low)
        if micro == micro_count - 1:
            ffn_low = after(ffn_low, up_sum[1])
        hidden_grad = contract_cols(ffn_low, full_down)
        pre_grad = gelu_back(pre, hidden_grad).astype(low)
        normed2_grad = contract_cols(pre_grad, full_up)
        resid_part, gain2_grad = norm_back(resid, gains[1], normed2_grad)
        resid_grad = after_grad + resid_part
        attn_low = resid_grad.astype(low)
        kept_dense.append((normed2, pre_grad, hidden, ffn_low))
        resid_grads.append((resid_grad, attn_low, gain2_grad))

    def run_attend_back(micro):
        inputs, normed, whole, mixed = dense[micro][:4]
        resid_grad, attn_low, gain2_grad = resid_grads[micro]
        mixed_grad = contract_cols(attn_low, full_mix).astype(low)
        mixed_grad = mixed_grad.reshape(rows_dev, dp_count, mine).transpose(1, 0, 2)
        mixed_grad = swap_heads(mixed_grad).reshape(length, mine)
        if micro == micro_count - 1:
            joined = [jnp.concatenate(parts, 0) for parts in zip(*kept_dense)]
            down_start = scatter_start(contract_rows(joined[2], joined[3]).astype(low), order_c)
            up_low = contract_rows(joined[0], joined[1]).astype(low)
            mixed_grad = after(mixed_grad, down_start[0], up_low, down_sum[0])
            late.extend((down_start, up_low))
        whole_grad = attend_back(whole, mixed_grad, prefix[micro], block)
        whole_grads.append(whole_grad)
        qkv_grad = swap_heads(whole_grad.reshape(dp_count, rows_dev, 3 * mine))
        qkv_grad = qkv_grad.transpose(1, 0, 2).reshape(rows_dev, 3 * width)
        if micro == micro_count - 1:
            qkv_grad = after(qkv_grad, up_sum[0])
        normed_grad = contract_cols(qkv_grad, full_qkv)
        input_part, gain1_grad = norm_back(inputs, gains[0], normed_grad)
        input_grads.append(resid_grad + input_part)
        gain_sums.append(jnp.stack([gain1_grad, gain2_grad]))
        kept.append((normed, qkv_grad, mixed, attn_low))

    last = micro_count - 1
    for micro in micros:
        if micro < last:
            run_second(micro, mixes[micro + 1])
            run_third(micro, sends[micro + 1])
            run_own(micro)
            run_ffn_back(micro)
        else:
            run_second(micro, *(resid_grads[-1][1:2] if micro else ()))
    for micro in micros[:-1]:
        run_attend_back(micro)
    up_grads, down_grads = ([None, None], [None, None])
    by_stage = list(zip(*second_stage))
    down_grads[1] = grad_halves(by_stage[5], by_stage[6], True)
    up_grads[1] = grad_halves(by_stage[4], by_stage[7], False)
    run_third(last, up_grads[1], down_grads[1], *whole_grads)
    by_first, by_third = (list(zip(*first_stage)), list(zip(*third_stage)))
    down_grads[0] = grad_halves(by_first[4], by_third[1], True)
    up_grads[0] = grad_halves(by_first[2], by_third[2], False)
    down_sum, up_sum = ([None, None], [None, None])
    for layer in (1, 0):
        down_sum[layer] = scatter_near(down_grads[layer]).astype(f32)
        up_sum[layer] = scatter_near(up_grads[layer]).astype(f32)
    run_own(last, down_sum[1])
    run_ffn_back(last)
    run_attend_back(last)
    down_start, up_low = late
    gain_acc, gain_one = (sum(gain_sums), sum(gain_ones))
    joined = [jnp.concatenate(parts, 0) for parts in zip(*kept)]
    down_out = scatter_end(down_start)
    up_out = scatter_rows(up_low, order_d)
    mix_out = scatter_rows(contract_rows(joined[2], joined[3]).astype(low), order_d)
    qkv_low = contract_rows(joined[0], joined[1]).astype(low)
    qkv_out = jnp.concatenate(
        [scatter_rows(qkv_low[:, :half], order_c), scatter_rows(qkv_low[:, half:], order_d)], 1
    )
    qkv_out = (
        qkv_out.reshape(rows_qkv, dp_count, 3, mine)
        .transpose(0, 2, 1, 3)
        .reshape(rows_qkv, 3 * width)
    )

    output_list = []
    stat_list = []
    for micro in micros:
        attn, ffn, dense_out = (dense[micro][i] for i in (4, 6, 10))
        returned = swap_experts(branches[micro])
        branch = contract_rows(places[micro], returned)
        final = dense_out + branch
        output_list.append(final.astype(low))
        stat_list.append(jnp.stack([jnp.sum(v * v) for v in (final, attn, ffn, branch)]))

    small = jnp.concatenate(
        [
            jnp.stack(stat_list, 1).reshape(-1),
            sum(part[1] for part in own_grads),
            sum(part[2] for part in own_grads),
            0.5 * gain_one,
        ]
    )
    small = sum_small(small)
    stats = 4 * micro_count
    branch_rms = jnp.sqrt(small[:stats] / (length * width)).reshape(4, micro_count, 1)
    ex_gain = jnp.stack([small[stats : stats + width], small[stats + 2 * width :]])
    gain_sum = sum_small(gain_acc)
    for bit in order_a:
        gain_sum = gain_sum + swap(gain_sum, bit)
    device = lax.axis_index("dp") * experts + lax.axis_index("expert")
    gain_out = lax.dynamic_index_in_dim(
        gain_sum.reshape(2, dp_count * experts, -1), device, 1, keepdims=False
    )
    return (
        jnp.stack(output_list)[:, None],
        jnp.stack(input_grads)[:, None],
        qkv_out,
        mix_out,
        up_out,
        down_out,
        gain_out,
        jnp.stack(up_sum)[None],
        jnp.stack(down_sum)[None],
        ex_gain[None],
        small[None, stats + width : stats + 2 * width],
        branch_rms,
    )


def solution(mesh):
    return jax.shard_map(
        shards,
        mesh=mesh,
        in_specs=(
            P(None, "expert", "dp", None),
            P(None, "expert", "dp", None),
            P(None, "expert", "dp", None),
            P(None, "expert"),
            P(("dp", "expert"), None),
            P(("dp", "expert"), None),
            P(("dp", "expert"), None),
            P(("dp", "expert"), None),
            P(None, ("dp", "expert")),
            P("expert", None, None, "dp"),
            P("expert", None, "dp", None),
            P("expert", None, None),
            P("expert", None),
        ),
        out_specs=(
            P(None, "expert", "dp", None),
            P(None, "expert", "dp", None),
            P(("dp", "expert"), None),
            P(("dp", "expert"), None),
            P(("dp", "expert"), None),
            P(("dp", "expert"), None),
            P(None, ("dp", "expert")),
            P("expert", None, None, "dp"),
            P("expert", None, "dp", None),
            P("expert", None, None),
            P("expert", None),
            P(None, None, "expert"),
        ),
        check_vma=False,
    )
```

```python
import functools

import jax
import jax.numpy as jnp
from jax import lax
from jax.experimental import pallas as pl
from jax.experimental.pallas import tpu as pltpu
from jax.sharding import PartitionSpec as P

HEAD_DIM = 64


eps = 1e-05


def layer_norm(values, gain):
    centred = values - jnp.mean(values, -1, keepdims=True)
    spread = jnp.mean(centred * centred, -1, keepdims=True)
    return centred * lax.rsqrt(spread + eps) * gain


def norm_back(values, gain, grads):
    _, pullback = jax.vjp(layer_norm, values, gain)
    return pullback(grads)


def gelu(values):
    return jax.nn.gelu(values, approximate=True)


def gelu_back(values, grads):
    _, pullback = jax.vjp(gelu, values)
    return pullback(grads)[0]


def contract_rows(left, right):
    return lax.dot_general(
        left, right, (((0,), (0,)), ((), ())), preferred_element_type=jnp.float32
    )


def contract_cols(left, right):
    return lax.dot_general(
        left, right, (((1,), (1,)), ((), ())), preferred_element_type=jnp.float32
    )


def swap(values, bit):
    count = lax.axis_size("expert")
    return lax.ppermute(values, "expert", [(i, i ^ bit) for i in range(count)])


def turn(values, shift):
    count = lax.axis_size("dp")
    return lax.ppermute(values, "dp", [(i, (i + shift) % count) for i in range(count)])


def sum_small(values):
    total = values
    for shift in range(1, lax.axis_size("dp")):
        total = total + turn(values, shift)
    return total


def bit_orders():
    count = lax.axis_size("expert")
    bits = [1 << i for i in range(count.bit_length() - 1)]
    upper = bits[1:]
    half = len(upper) // 2
    return upper[half:] + upper[:half] + bits[:1], upper[:half] + upper[half:] + bits[:1]


def assemble_kernel(masks, *refs):
    count = len(masks)
    pieces, full, held, in_sems, out_sems = (
        refs[:count],
        refs[count],
        refs[count + 1],
        refs[count + 2],
        refs[count + 3],
    )
    own = lax.axis_index("expert")
    loads = [pltpu.make_async_copy(pieces[i], held.at[i], in_sems.at[i]) for i in range(count)]
    stores = [
        pltpu.make_async_copy(
            held.at[i], full.at[:, jnp.bitwise_xor(own, mask)], out_sems.at[i]
        )
        for i, mask in enumerate(masks)
    ]
    for load in loads:
        load.start()
    for load, store in zip(loads, stores):
        load.wait()
        store.start()
    for store in stores:
        store.wait()


def assemble(pieces):
    masks = [mask for mask, _ in pieces]
    arrays = [piece for _, piece in pieces]
    dp_count, rows, cols = arrays[0].shape
    full = pl.pallas_call(
        functools.partial(assemble_kernel, masks),
        out_shape=jax.ShapeDtypeStruct((dp_count, len(masks), rows, cols), arrays[0].dtype),
        in_specs=[pl.BlockSpec(memory_space=pl.ANY)] * len(masks),
        out_specs=pl.BlockSpec(memory_space=pl.ANY),
        scratch_shapes=[
            pltpu.VMEM((len(masks), dp_count, rows, cols), arrays[0].dtype),
            pltpu.SemaphoreType.DMA((len(masks),)),
            pltpu.SemaphoreType.DMA((len(masks),)),
        ],
        name="assemble",
    )(*arrays)
    return full.reshape(dp_count * len(masks) * rows, cols)


def spread(piece, order):
    pieces = [(0, piece)]
    for bit in order:
        pieces = pieces + [(mask ^ bit, swap(part, bit)) for mask, part in pieces]
    return pieces


def gather_dp(shard):
    return lax.all_gather(shard, "dp", axis=0)


def turn_gather(shard):
    count = lax.axis_size("dp")
    own = lax.axis_index("dp")
    full = jnp.zeros((count,) + shard.shape, shard.dtype)
    for shift in range(count):
        part = shard if shift == 0 else turn(shard, shift)
        full = lax.dynamic_update_slice_in_dim(full, part[None], (own - shift) % count, 0)
    return full


def scatter_start(total, order):
    count = lax.axis_size("expert")
    dp_count = lax.axis_size("dp")
    rows = total.shape[0] // (count * dp_count)
    bits = sorted(order)
    current = total.reshape((dp_count,) + (2,) * len(bits) + (rows, total.shape[1]))
    left = sorted(bits, reverse=True)
    return scatter_bits(current, order[:1], left), order[1:], left


def scatter_bits(current, order, left):
    own = lax.axis_index("expert")
    for bit in order:
        axis = 1 + left.index(bit)
        mine = (own // bit) % 2
        send = lax.dynamic_index_in_dim(current, 1 - mine, axis, keepdims=False)
        keep = lax.dynamic_index_in_dim(current, mine, axis, keepdims=False)
        received = swap(send, bit)
        current = (keep.astype(jnp.float32) + received.astype(jnp.float32)).astype(jnp.bfloat16)
        left.remove(bit)
    return current


def scatter_middle(started):
    current, order, left = started
    current = scatter_bits(current, order, left)
    return current.reshape(-1, current.shape[-1])


def scatter_dp(total):
    return lax.psum_scatter(total, "dp", scatter_dimension=0, tiled=True).astype(jnp.float32)


def scatter_end(started):
    return scatter_dp(scatter_middle(started))


def scatter_rows(total, order):
    return scatter_end(scatter_start(total, order))


def swap_heads(blocks):
    return lax.all_to_all(blocks, "dp", split_axis=0, concat_axis=0, tiled=True)


def swap_experts(slots):
    count = lax.axis_size("expert")
    blocks = slots.reshape(count, -1, slots.shape[1])
    return lax.all_to_all(blocks, "expert", split_axis=0, concat_axis=0, tiled=True).reshape(
        slots.shape
    )


def head_probs(x_ref, query, allowed, width, h):
    keys = x_ref[:, width + h * HEAD_DIM : width + (h + 1) * HEAD_DIM]
    values = x_ref[:, 2 * width + h * HEAD_DIM : 2 * width + (h + 1) * HEAD_DIM]
    scores = jnp.where(allowed, contract_cols(keys, query), -1e30)
    top = jnp.max(scores, 0, keepdims=True)
    weights = jnp.exp(scores - top)
    return keys, values, weights, jnp.sum(weights, 0, keepdims=True)


def allowed_pairs(length, block, start, prefix):
    key_pos = lax.broadcasted_iota(jnp.int32, (length, block), 0)
    query_pos = start + lax.broadcasted_iota(jnp.int32, (length, block), 1)
    return (key_pos <= query_pos) | (key_pos < prefix)


def attend_kernel(prefix_ref, x_ref, out_ref):
    block, width = out_ref.shape
    length = x_ref.shape[0]
    start = pl.multiple_of(pl.program_id(0) * block, block)
    allowed = allowed_pairs(length, block, start, prefix_ref[0])
    query = x_ref[pl.ds(start, block), :width]
    parts = []
    for h in range(width // HEAD_DIM):
        own = query[:, h * HEAD_DIM : (h + 1) * HEAD_DIM] * HEAD_DIM ** (-0.5)
        _, values, weights, total = head_probs(x_ref, own, allowed, width, h)
        parts.append(contract_rows(values, weights.astype(jnp.bfloat16)) * (1.0 / total))
    out_ref[...] = jnp.concatenate(parts, 0).T.astype(out_ref.dtype)


def attend_cost(length, cols, products):
    return pl.CostEstimate(
        flops=products * length * length * cols // 3,
        transcendentals=length * length * cols // (3 * HEAD_DIM),
        bytes_accessed=products * length * cols,
    )


def attend(whole, prefix, block):
    length, cols = whole.shape
    width = cols // 3
    return pl.pallas_call(
        attend_kernel,
        out_shape=jax.ShapeDtypeStruct((length, width), whole.dtype),
        grid=(length // block,),
        in_specs=[
            pl.BlockSpec(memory_space=pltpu.SMEM),
            pl.BlockSpec((length, cols), lambda i: (0, 0)),
        ],
        out_specs=pl.BlockSpec((block, width), lambda i: (i, 0)),
        cost_estimate=attend_cost(length, cols, 4),
        name="attend",
    )(prefix, whole)


def attend_back_kernel(prefix_ref, x_ref, grad_ref, out_ref, key_acc, value_acc):
    block, width = grad_ref.shape
    length = x_ref.shape[0]
    step = pl.program_id(0)
    start = pl.multiple_of(step * block, block)
    allowed = allowed_pairs(length, block, start, prefix_ref[0])
    query = x_ref[pl.ds(start, block), :width]
    heads = width // HEAD_DIM

    @pl.when(step == 0)
    def _():
        key_acc[...] = jnp.zeros_like(key_acc)
        value_acc[...] = jnp.zeros_like(value_acc)

    parts = []
    for h in range(heads):
        own = query[:, h * HEAD_DIM : (h + 1) * HEAD_DIM] * HEAD_DIM ** (-0.5)
        grad = grad_ref[:, h * HEAD_DIM : (h + 1) * HEAD_DIM]
        keys, values, weights, total = head_probs(x_ref, own, allowed, width, h)
        probs = weights * (1.0 / total)
        prob_grad = contract_cols(values, grad)
        inner = jnp.sum(probs * prob_grad, 0, keepdims=True)
        score_grad = (probs * (prob_grad - inner)).astype(jnp.bfloat16)
        value_acc[h] += jnp.dot(
            probs.astype(jnp.bfloat16), grad, preferred_element_type=jnp.float32
        )
        key_acc[h] += jnp.dot(score_grad, own, preferred_element_type=jnp.float32)
        parts.append(contract_rows(keys, score_grad) * HEAD_DIM ** (-0.5))
    out_ref[pl.ds(start, block), :width] = jnp.concatenate(parts, 0).T.astype(out_ref.dtype)

    @pl.when(step == pl.num_programs(0) - 1)
    def _():
        out_ref[:, width : 2 * width] = jnp.concatenate(
            [key_acc[h] for h in range(heads)], 1
        ).astype(out_ref.dtype)
        out_ref[:, 2 * width :] = jnp.concatenate(
            [value_acc[h] for h in range(heads)], 1
        ).astype(out_ref.dtype)


def attend_back(whole, grads, prefix, block):
    length, cols = whole.shape
    width = cols // 3
    heads = width // HEAD_DIM
    return pl.pallas_call(
        attend_back_kernel,
        out_shape=jax.ShapeDtypeStruct((length, cols), whole.dtype),
        grid=(length // block,),
        in_specs=[
            pl.BlockSpec(memory_space=pltpu.SMEM),
            pl.BlockSpec((length, cols), lambda i: (0, 0)),
            pl.BlockSpec((block, width), lambda i: (i, 0)),
        ],
        out_specs=pl.BlockSpec((length, cols), lambda i: (0, 0)),
        scratch_shapes=[
            pltpu.VMEM((heads, length, HEAD_DIM), jnp.float32),
            pltpu.VMEM((heads, length, HEAD_DIM), jnp.float32),
        ],
        cost_estimate=attend_cost(length, cols, 10),
        name="attend_back",
    )(prefix, whole, grads)


def after(value, *others):
    return lax.optimization_barrier((value,) + others)[0]


def flip(values, bit):
    count = lax.axis_size("dp")
    return lax.ppermute(values, "dp", [(i, i ^ bit) for i in range(count)])


def near_groups():
    count = lax.axis_size("dp")
    return [[i, i ^ 1] for i in range(count) if not i & 1]


def gather_near(shard):
    return lax.all_gather(shard, "dp", axis=0, axis_index_groups=near_groups())


def scatter_near(parts):
    shape = parts.shape[1:]
    total = lax.psum_scatter(
        parts.reshape(-1, shape[-1]),
        "dp",
        scatter_dimension=0,
        axis_index_groups=near_groups(),
        tiled=True,
    )
    return total.reshape(shape)


def both_rows(own):
    return jnp.concatenate([own, flip(own, 2)], 0)


def sum_pair(partial_sums):
    size = partial_sums.shape[0] // 2
    received = flip(partial_sums, 2)
    return partial_sums.astype(jnp.float32) + jnp.concatenate(
        [received[size:], received[:size]], 0
    ).astype(jnp.float32)


def sum_own(partial_sums):
    size = partial_sums.shape[0] // 2
    received = flip(partial_sums[size:], 2)
    return partial_sums[:size].astype(jnp.float32) + received.astype(jnp.float32)


def shards(
    tokens,
    cotangent,
    routes,
    prefix,
    qkv_weight,
    mix_weight,
    up_weight,
    down_weight,
    dense_gain,
    expert_up,
    expert_down,
    expert_gain,
    centroids,
):
    f32, low = jnp.float32, jnp.bfloat16
    micro_count, _, rows_dev, width = tokens.shape
    dp_count = lax.axis_size("dp")
    experts = lax.axis_size("expert")
    capacity = max(2, 5 * rows_dev // (4 * experts))
    length = rows_dev * dp_count
    mine = width // dp_count
    block = min(256, length)
    micros = range(micro_count)
    slot_ids = jnp.arange(experts * capacity, dtype=jnp.int32)
    expert_ids = jnp.arange(experts, dtype=jnp.int32)
    up_ex, down_ex, centroid = (expert_up[0], expert_down[0], centroids[0])
    gain_ex = expert_gain[0].astype(f32)

    places, grad_rows = ([], [])
    for micro in micros:
        route = routes[micro, 0, :, 0]
        onehot = (route[:, None] == expert_ids[None, :]).astype(jnp.int32)
        rank = jnp.sum((jnp.cumsum(onehot, 0) - 1) * onehot, 1)
        slot = route * capacity + rank
        place = (slot[None, :] == slot_ids[:, None]).astype(low)
        places.append(place)
        grad_sent = jnp.dot(
            place, cotangent[micro, 0].astype(low), preferred_element_type=f32
        ).astype(low)
        grad_rows.append(both_rows(swap_experts(grad_sent)))

    order_a, order_b = bit_orders()
    rows_qkv = qkv_weight.shape[0]
    by_dest = (
        qkv_weight.reshape(rows_qkv, 3, dp_count, mine)
        .transpose(0, 2, 1, 3)
        .reshape(rows_qkv, 3 * width)
    )
    half = 3 * width // 2
    gain_cols = jnp.pad(dense_gain.T, ((0, 0), (0, 126)))
    first = turn_gather(jnp.concatenate([by_dest, gain_cols], 1))
    part_a = spread(first[:, :, :half], order_a)
    part_b = spread(first[:, :, half:], order_b)
    qkv_pieces = dict(part_b)
    full_qkv = assemble(
        [(mask, jnp.concatenate([piece, qkv_pieces[mask][:, :, :half]], 2)) for mask, piece in part_a]
    )
    mix_dp = turn_gather(mix_weight)
    full_qkv = after(full_qkv, mix_dp)
    full_gain = assemble([(mask, piece[:, :, half:]) for mask, piece in part_b])
    gains = full_gain[:, :2].T.astype(f32)
    full_mix = assemble(spread(mix_dp, order_a))
    up_pieces = spread(gather_dp(up_weight), order_a)
    down_pieces = spread(gather_dp(down_weight), order_b)
    full_up, full_down = (assemble(up_pieces), assemble(down_pieces))
    hops = [
        [piece for pieces in (up_pieces, down_pieces) for _, piece in pieces[start : 2 * start]]
        for start in (1, 2)
    ]

    up_both, down_both = ([], [])
    for layer in range(2):
        up_near = gather_near(after(up_ex[layer], first))
        up_both.append(jnp.concatenate([up_near[0], up_near[1]], 1))
        down_both.append(gather_near(after(down_ex[layer], first)).reshape(-1, width))

    dense = []
    slots_in = []
    sends, mixes = ([], [])
    for micro in micros:
        source = tokens[micro, 0]
        if micro > 0:
            source = after(source, slots_in[micro - 1])
        inputs = source.astype(f32)
        normed = layer_norm(inputs, gains[0]).astype(low)
        qkv = jnp.dot(normed, full_qkv, preferred_element_type=f32).astype(low)
        blocks = qkv.reshape(rows_dev, dp_count, 3 * mine).transpose(1, 0, 2)
        whole = swap_heads(blocks).reshape(length, 3 * mine)
        if micro == 0:
            whole = after(whole, *hops[0])
        mixed = attend(whole, prefix[micro], block).reshape(dp_count, rows_dev, mine)
        mixed = swap_heads(mixed)
        mixes.append(mixed)
        if micro == 0:
            mixed = after(mixed, *hops[1])
        mixed = mixed.transpose(1, 0, 2).reshape(rows_dev, width)
        attn = jnp.dot(mixed, full_mix, preferred_element_type=f32)
        resid = inputs + attn
        normed2 = layer_norm(resid, gains[1]).astype(low)
        pre = jnp.dot(normed2, full_up, preferred_element_type=f32)
        hidden = gelu(pre).astype(low)
        ffn = jnp.dot(hidden, full_down, preferred_element_type=f32)
        dense_out = resid + ffn
        sent = jnp.dot(places[micro], dense_out.astype(low), preferred_element_type=f32).astype(low)
        dense.append((inputs, normed, whole, mixed, attn, resid, ffn, normed2, pre, hidden, dense_out))
        sends.append(sent)
        slots_in.append(swap_experts(sent))

    slot_count = experts * capacity
    first_stage = []
    for micro in micros:
        rows = both_rows(slots_in[micro])
        if micro > 0:
            rows = after(rows, first_stage[micro - 1][-1])
        sig = jax.nn.sigmoid(jnp.dot(rows, centroid, preferred_element_type=f32))[:, None]
        state0 = rows.astype(f32)
        z0 = layer_norm(state0, gain_ex[0]).astype(low)
        pre0 = jnp.dot(z0, up_both[0], preferred_element_type=f32)
        h0 = gelu(pre0).astype(low)
        out0 = jnp.dot(h0, down_both[0], preferred_element_type=f32).astype(low)
        first_stage.append((rows, sig, z0, pre0, h0, out0))
    second_stage = []

    def run_second(micro, *others):
        rows, sig = first_stage[micro][:2]
        total = sum_pair(first_stage[micro][-1])
        total = after(total, *others)
        state1 = rows.astype(f32) + total
        z1 = layer_norm(state1, gain_ex[1]).astype(low)
        pre1 = jnp.dot(z1, up_both[1], preferred_element_type=f32)
        h1 = gelu(pre1).astype(low)
        out1 = jnp.dot(h1, down_both[1], preferred_element_type=f32).astype(low)
        incoming = grad_rows[micro].astype(f32)
        grad2 = incoming * sig
        grad_y = grad2.astype(low)
        pre_grad = gelu_back(pre1, contract_cols(grad_y, down_both[1])).astype(low)
        normed_part = contract_cols(pre_grad, up_both[1]).astype(low)
        second_stage.append((state1, out1, incoming, grad2, z1, h1, grad_y, pre_grad, normed_part))

    hidden_dev = up_ex.shape[2]
    hidden_halves = (slice(0, hidden_dev), slice(hidden_dev, 2 * hidden_dev))

    def grad_halves(lefts, rights, split_left):
        left, right = (jnp.concatenate(parts, 0) for parts in (lefts, rights))
        return [
            contract_rows(left[:, half] if split_left else left, right if split_left else right[:, half])
            for half in hidden_halves
        ]

    def join_halves(down_parts, up_parts):
        return jnp.stack([jnp.stack(parts) for parts in zip(down_parts, up_parts)]).astype(low)

    gain_ones = []
    third_stage = []

    def run_third(micro, *others):
        rows, sig, z0, pre0, h0, _ = first_stage[micro]
        state1, out1, incoming, grad2 = second_stage[micro][:4]
        total = sum_pair(second_stage[micro][-1])
        total = after(total, *others)
        state_grad, gain_grad = norm_back(state1, gain_ex[1], total)
        grad1 = grad2 + state_grad
        grad_y = grad1.astype(low)
        pre_grad = gelu_back(pre0, contract_cols(grad_y, down_both[0])).astype(low)
        normed_part = contract_cols(pre_grad, up_both[0]).astype(low)
        third_stage.append((grad1, grad_y, pre_grad, normed_part))
        gain_ones.append(gain_grad)
    own_grads = []
    branches = []

    def run_own(micro, *others):
        rows, sig = first_stage[micro][:2]
        state1, out1, incoming = second_stage[micro][:3]
        grad1, normed_part = (third_stage[micro][i] for i in (0, 3))
        normed_grad = after(sum_own(normed_part), *others)
        own_rows = rows[:slot_count].astype(f32)
        state_grad, gain_grad = norm_back(own_rows, gain_ex[0], normed_grad)
        own_sig = sig[:slot_count]
        state2 = state1[:slot_count] + sum_own(out1)
        branches.append((own_sig * state2).astype(low))
        score_grad = jnp.sum(incoming[:slot_count] * state2, 1, keepdims=True)
        score_grad = score_grad * own_sig * (1.0 - own_sig)
        row_grad = grad1[:slot_count] + state_grad + score_grad * centroid.astype(f32)
        cent_grad = jnp.sum(score_grad * own_rows, 0)
        own_grads.append((row_grad.astype(low), gain_grad, cent_grad))

    gain_sums, resid_grads, late = ([], [], [])
    input_grads = []
    kept = []
    kept_dense = []
    order_c, order_d = (order_a[::-1], order_b[::-1])
    whole_grads = []

    def run_ffn_back(micro):
        inputs, normed, whole, mixed, attn, resid, ffn, normed2, pre, hidden, _ = dense[micro]
        grad_back = swap_experts(own_grads[micro][0])
        after_grad = cotangent[micro, 0] + contract_rows(places[micro], grad_back)
        ffn_low = after_grad.astype(low)
        if micro == micro_count - 1:
            ffn_low, layer_sums[1] = lax.optimization_barrier((ffn_low, layer_sums[1]))
            ffn_low = after(ffn_low, *(terms[1] for terms in kept))
        hidden_grad = contract_cols(ffn_low, full_down)
        pre_grad = gelu_back(pre, hidden_grad).astype(low)
        normed2_grad = contract_cols(pre_grad, full_up)
        resid_part, gain2_grad = norm_back(resid, gains[1], normed2_grad)
        resid_grad = after_grad + resid_part
        attn_low = resid_grad.astype(low)
        kept_dense.append((normed2, pre_grad, hidden, ffn_low))
        resid_grads.append((resid_grad, attn_low, gain2_grad))

    def run_attend_back(micro):
        inputs, normed, whole, mixed = dense[micro][:4]
        resid_grad, attn_low, gain2_grad = resid_grads[micro]
        mixed_grad = contract_cols(attn_low, full_mix).astype(low)
        mixed_grad = mixed_grad.reshape(rows_dev, dp_count, mine).transpose(1, 0, 2)
        mixed_grad = swap_heads(mixed_grad).reshape(length, mine)
        if micro == micro_count - 1:
            joined = [jnp.concatenate(parts, 0) for parts in zip(*kept_dense)]
            down_start = scatter_start(contract_rows(joined[2], joined[3]).astype(low), order_c)
            up_low = contract_rows(joined[0], joined[1]).astype(low)
            mixed_grad = after(mixed_grad, down_start[0], up_low)
            late.extend((down_start, up_low))
        whole_grad = attend_back(whole, mixed_grad, prefix[micro], block)
        whole_grads.append(whole_grad)
        qkv_grad = swap_heads(whole_grad.reshape(dp_count, rows_dev, 3 * mine))
        qkv_grad = qkv_grad.transpose(1, 0, 2).reshape(rows_dev, 3 * width)
        if micro == micro_count - 1:
            qkv_grad, layer_sums[0] = lax.optimization_barrier((qkv_grad, layer_sums[0]))
        normed_grad = contract_cols(qkv_grad, full_qkv)
        input_part, gain1_grad = norm_back(inputs, gains[0], normed_grad)
        input_grads.append(resid_grad + input_part)
        gain_sums.append(jnp.stack([gain1_grad, gain2_grad]))
        kept.append((normed, qkv_grad, mixed, attn_low))

    last = micro_count - 1
    for micro in micros:
        if micro < last:
            run_second(micro, mixes[micro + 1])
            run_third(micro, sends[micro + 1])
            run_own(micro)
            run_ffn_back(micro)
        else:
            run_second(micro, *(resid_grads[-1][1:2] if micro else ()))
    for micro in micros[:-1]:
        run_attend_back(micro)
    layer_grads, layer_sums = ([None, None], [None, None])
    by_stage = list(zip(*second_stage))
    layer_grads[1] = join_halves(
        grad_halves(by_stage[5], by_stage[6], True), grad_halves(by_stage[4], by_stage[7], False)
    )
    run_third(last, layer_grads[1], *whole_grads)
    by_first, by_third = (list(zip(*first_stage)), list(zip(*third_stage)))
    layer_grads[0] = join_halves(
        grad_halves(by_first[4], by_third[1], True), grad_halves(by_first[2], by_third[2], False)
    )
    for layer in (1, 0):
        layer_sums[layer] = scatter_near(layer_grads[layer])
    run_own(last)
    run_ffn_back(last)
    run_attend_back(last)
    down_start, up_low = late
    down_sum, up_sum = ([total[i].astype(f32) for total in layer_sums] for i in range(2))
    gain_acc, gain_one = (sum(gain_sums), sum(gain_ones))
    joined = [jnp.concatenate(parts, 0) for parts in zip(*kept)]
    down_out = scatter_end(down_start)
    up_out = scatter_rows(up_low, order_d)
    mix_low = contract_rows(joined[2], joined[3]).astype(low)
    qkv_low = contract_rows(joined[0], joined[1]).astype(low)
    qkv_mix = scatter_dp(
        jnp.concatenate(
            [
                scatter_middle(scatter_start(part, order))
                for part, order in (
                    (qkv_low[:, :half], order_c),
                    (qkv_low[:, half:], order_d),
                    (mix_low, order_d),
                )
            ],
            1,
        )
    )
    mix_out = qkv_mix[:, 3 * width :]
    qkv_out = (
        qkv_mix[:, : 3 * width].reshape(rows_qkv, dp_count, 3, mine)
        .transpose(0, 2, 1, 3)
        .reshape(rows_qkv, 3 * width)
    )

    output_list = []
    stat_list = []
    for micro in micros:
        attn, ffn, dense_out = (dense[micro][i] for i in (4, 6, 10))
        returned = swap_experts(branches[micro])
        branch = contract_rows(places[micro], returned)
        final = dense_out + branch
        output_list.append(final.astype(low))
        stat_list.append(jnp.stack([jnp.sum(v * v) for v in (final, attn, ffn, branch)]))

    small = jnp.concatenate(
        [
            jnp.stack(stat_list, 1).reshape(-1),
            sum(part[1] for part in own_grads),
            sum(part[2] for part in own_grads),
            0.5 * gain_one,
        ]
    )
    small = sum_small(small)
    stats = 4 * micro_count
    branch_rms = jnp.sqrt(small[:stats] / (length * width)).reshape(4, micro_count, 1)
    ex_gain = jnp.stack([small[stats : stats + width], small[stats + 2 * width :]])
    gain_sum = sum_small(gain_acc)
    for bit in order_a:
        gain_sum = gain_sum + swap(gain_sum, bit)
    device = lax.axis_index("dp") * experts + lax.axis_index("expert")
    gain_out = lax.dynamic_index_in_dim(
        gain_sum.reshape(2, dp_count * experts, -1), device, 1, keepdims=False
    )
    return (
        jnp.stack(output_list)[:, None],
        jnp.stack(input_grads)[:, None],
        qkv_out,
        mix_out,
        up_out,
        down_out,
        gain_out,
        jnp.stack(up_sum)[None],
        jnp.stack(down_sum)[None],
        ex_gain[None],
        small[None, stats + width : stats + 2 * width],
        branch_rms,
    )


def solution(mesh):
    return jax.shard_map(
        shards,
        mesh=mesh,
        in_specs=(
            P(None, "expert", "dp", None),
            P(None, "expert", "dp", None),
            P(None, "expert", "dp", None),
            P(None, "expert"),
            P(("dp", "expert"), None),
            P(("dp", "expert"), None),
            P(("dp", "expert"), None),
            P(("dp", "expert"), None),
            P(None, ("dp", "expert")),
            P("expert", None, None, "dp"),
            P("expert", None, "dp", None),
            P("expert", None, None),
            P("expert", None),
        ),
        out_specs=(
            P(None, "expert", "dp", None),
            P(None, "expert", "dp", None),
            P(("dp", "expert"), None),
            P(("dp", "expert"), None),
            P(("dp", "expert"), None),
            P(("dp", "expert"), None),
            P(None, ("dp", "expert")),
            P("expert", None, None, "dp"),
            P("expert", None, "dp", None),
            P("expert", None, None),
            P("expert", None),
            P(None, None, "expert"),
        ),
        check_vma=False,
    )
```

```python
import functools

import jax
import jax.numpy as jnp
from jax import lax
from jax.experimental import pallas as pl
from jax.experimental.pallas import tpu as pltpu
from jax.sharding import PartitionSpec as P

HEAD_DIM = 64


eps = 1e-05


def layer_norm(values, gain):
    centred = values - jnp.mean(values, -1, keepdims=True)
    spread = jnp.mean(centred * centred, -1, keepdims=True)
    return centred * lax.rsqrt(spread + eps) * gain


def norm_back(values, gain, grads):
    _, pullback = jax.vjp(layer_norm, values, gain)
    return pullback(grads)


def gelu(values):
    return jax.nn.gelu(values, approximate=True)


def gelu_back(values, grads):
    _, pullback = jax.vjp(gelu, values)
    return pullback(grads)[0]


def contract_rows(left, right):
    return lax.dot_general(
        left, right, (((0,), (0,)), ((), ())), preferred_element_type=jnp.float32
    )


def contract_cols(left, right):
    return lax.dot_general(
        left, right, (((1,), (1,)), ((), ())), preferred_element_type=jnp.float32
    )


def swap(values, bit):
    count = lax.axis_size("expert")
    return lax.ppermute(values, "expert", [(i, i ^ bit) for i in range(count)])


def turn(values, shift):
    count = lax.axis_size("dp")
    return lax.ppermute(values, "dp", [(i, (i + shift) % count) for i in range(count)])


def sum_small(values):
    total = values
    for shift in range(1, lax.axis_size("dp")):
        total = total + turn(values, shift)
    return total


def bit_orders():
    count = lax.axis_size("expert")
    bits = [1 << i for i in range(count.bit_length() - 1)]
    upper = bits[1:]
    half = len(upper) // 2
    return upper[half:] + upper[:half] + bits[:1], upper[:half] + upper[half:] + bits[:1]


def assemble_kernel(masks, *refs):
    count = len(masks)
    pieces, full, held, in_sems, out_sems = (
        refs[:count],
        refs[count],
        refs[count + 1],
        refs[count + 2],
        refs[count + 3],
    )
    own = lax.axis_index("expert")
    loads = [pltpu.make_async_copy(pieces[i], held.at[i], in_sems.at[i]) for i in range(count)]
    stores = [
        pltpu.make_async_copy(
            held.at[i], full.at[:, jnp.bitwise_xor(own, mask)], out_sems.at[i]
        )
        for i, mask in enumerate(masks)
    ]
    for load in loads:
        load.start()
    for load, store in zip(loads, stores):
        load.wait()
        store.start()
    for store in stores:
        store.wait()


def assemble(pieces):
    masks = [mask for mask, _ in pieces]
    arrays = [piece for _, piece in pieces]
    dp_count, rows, cols = arrays[0].shape
    full = pl.pallas_call(
        functools.partial(assemble_kernel, masks),
        out_shape=jax.ShapeDtypeStruct((dp_count, len(masks), rows, cols), arrays[0].dtype),
        in_specs=[pl.BlockSpec(memory_space=pl.ANY)] * len(masks),
        out_specs=pl.BlockSpec(memory_space=pl.ANY),
        scratch_shapes=[
            pltpu.VMEM((len(masks), dp_count, rows, cols), arrays[0].dtype),
            pltpu.SemaphoreType.DMA((len(masks),)),
            pltpu.SemaphoreType.DMA((len(masks),)),
        ],
        name="assemble",
    )(*arrays)
    return full.reshape(dp_count * len(masks) * rows, cols)


def spread(piece, order):
    pieces = [(0, piece)]
    for bit in order:
        pieces = pieces + [(mask ^ bit, swap(part, bit)) for mask, part in pieces]
    return pieces


def gather_dp(shard):
    return lax.all_gather(shard, "dp", axis=0)


def turn_gather(shard):
    count = lax.axis_size("dp")
    own = lax.axis_index("dp")
    full = jnp.zeros((count,) + shard.shape, shard.dtype)
    for shift in range(count):
        part = shard if shift == 0 else turn(shard, shift)
        full = lax.dynamic_update_slice_in_dim(full, part[None], (own - shift) % count, 0)
    return full


def scatter_start(total, order):
    count = lax.axis_size("expert")
    dp_count = lax.axis_size("dp")
    rows = total.shape[0] // (count * dp_count)
    bits = sorted(order)
    current = total.reshape((dp_count,) + (2,) * len(bits) + (rows, total.shape[1]))
    left = sorted(bits, reverse=True)
    return scatter_bits(current, order[:1], left), order[1:], left


def scatter_bits(current, order, left):
    own = lax.axis_index("expert")
    for bit in order:
        axis = 1 + left.index(bit)
        mine = (own // bit) % 2
        send = lax.dynamic_index_in_dim(current, 1 - mine, axis, keepdims=False)
        keep = lax.dynamic_index_in_dim(current, mine, axis, keepdims=False)
        received = swap(send, bit)
        current = (keep.astype(jnp.float32) + received.astype(jnp.float32)).astype(jnp.bfloat16)
        left.remove(bit)
    return current


def scatter_middle(started):
    current, order, left = started
    current = scatter_bits(current, order, left)
    return current.reshape(-1, current.shape[-1])


def scatter_dp(total):
    return lax.psum_scatter(total, "dp", scatter_dimension=0, tiled=True).astype(jnp.float32)


def scatter_end(started):
    return scatter_dp(scatter_middle(started))


def scatter_rows(total, order):
    return scatter_end(scatter_start(total, order))


def swap_heads(blocks):
    return lax.all_to_all(blocks, "dp", split_axis=0, concat_axis=0, tiled=True)


def swap_experts(slots):
    count = lax.axis_size("expert")
    blocks = slots.reshape(count, -1, slots.shape[1])
    return lax.all_to_all(blocks, "expert", split_axis=0, concat_axis=0, tiled=True).reshape(
        slots.shape
    )


def head_probs(x_ref, query, allowed, width, h):
    keys = x_ref[:, width + h * HEAD_DIM : width + (h + 1) * HEAD_DIM]
    values = x_ref[:, 2 * width + h * HEAD_DIM : 2 * width + (h + 1) * HEAD_DIM]
    scores = jnp.where(allowed, contract_cols(keys, query), -1e30)
    top = jnp.max(scores, 0, keepdims=True)
    weights = jnp.exp(scores - top)
    return keys, values, weights, jnp.sum(weights, 0, keepdims=True)


def allowed_pairs(length, block, start, prefix):
    key_pos = lax.broadcasted_iota(jnp.int32, (length, block), 0)
    query_pos = start + lax.broadcasted_iota(jnp.int32, (length, block), 1)
    return (key_pos <= query_pos) | (key_pos < prefix)


def attend_kernel(prefix_ref, x_ref, out_ref):
    block, width = out_ref.shape
    length = x_ref.shape[0]
    start = pl.multiple_of(pl.program_id(0) * block, block)
    allowed = allowed_pairs(length, block, start, prefix_ref[0])
    query = x_ref[pl.ds(start, block), :width]
    parts = []
    for h in range(width // HEAD_DIM):
        own = query[:, h * HEAD_DIM : (h + 1) * HEAD_DIM] * HEAD_DIM ** (-0.5)
        _, values, weights, total = head_probs(x_ref, own, allowed, width, h)
        parts.append(contract_rows(values, weights.astype(jnp.bfloat16)) * (1.0 / total))
    out_ref[...] = jnp.concatenate(parts, 0).T.astype(out_ref.dtype)


def attend_cost(length, cols, products):
    return pl.CostEstimate(
        flops=products * length * length * cols // 3,
        transcendentals=length * length * cols // (3 * HEAD_DIM),
        bytes_accessed=products * length * cols,
    )


def attend(whole, prefix, block):
    length, cols = whole.shape
    width = cols // 3
    return pl.pallas_call(
        attend_kernel,
        out_shape=jax.ShapeDtypeStruct((length, width), whole.dtype),
        grid=(length // block,),
        in_specs=[
            pl.BlockSpec(memory_space=pltpu.SMEM),
            pl.BlockSpec((length, cols), lambda i: (0, 0)),
        ],
        out_specs=pl.BlockSpec((block, width), lambda i: (i, 0)),
        cost_estimate=attend_cost(length, cols, 4),
        name="attend",
    )(prefix, whole)


def attend_back_kernel(prefix_ref, x_ref, grad_ref, out_ref, key_acc, value_acc):
    block, width = grad_ref.shape
    length = x_ref.shape[0]
    step = pl.program_id(0)
    start = pl.multiple_of(step * block, block)
    allowed = allowed_pairs(length, block, start, prefix_ref[0])
    query = x_ref[pl.ds(start, block), :width]
    heads = width // HEAD_DIM

    @pl.when(step == 0)
    def _():
        key_acc[...] = jnp.zeros_like(key_acc)
        value_acc[...] = jnp.zeros_like(value_acc)

    parts = []
    for h in range(heads):
        own = query[:, h * HEAD_DIM : (h + 1) * HEAD_DIM] * HEAD_DIM ** (-0.5)
        grad = grad_ref[:, h * HEAD_DIM : (h + 1) * HEAD_DIM]
        keys, values, weights, total = head_probs(x_ref, own, allowed, width, h)
        probs = weights * (1.0 / total)
        prob_grad = contract_cols(values, grad)
        inner = jnp.sum(probs * prob_grad, 0, keepdims=True)
        score_grad = (probs * (prob_grad - inner)).astype(jnp.bfloat16)
        value_acc[h] += jnp.dot(
            probs.astype(jnp.bfloat16), grad, preferred_element_type=jnp.float32
        )
        key_acc[h] += jnp.dot(score_grad, own, preferred_element_type=jnp.float32)
        parts.append(contract_rows(keys, score_grad) * HEAD_DIM ** (-0.5))
    out_ref[pl.ds(start, block), :width] = jnp.concatenate(parts, 0).T.astype(out_ref.dtype)

    @pl.when(step == pl.num_programs(0) - 1)
    def _():
        out_ref[:, width : 2 * width] = jnp.concatenate(
            [key_acc[h] for h in range(heads)], 1
        ).astype(out_ref.dtype)
        out_ref[:, 2 * width :] = jnp.concatenate(
            [value_acc[h] for h in range(heads)], 1
        ).astype(out_ref.dtype)


def attend_back(whole, grads, prefix, block):
    length, cols = whole.shape
    width = cols // 3
    heads = width // HEAD_DIM
    return pl.pallas_call(
        attend_back_kernel,
        out_shape=jax.ShapeDtypeStruct((length, cols), whole.dtype),
        grid=(length // block,),
        in_specs=[
            pl.BlockSpec(memory_space=pltpu.SMEM),
            pl.BlockSpec((length, cols), lambda i: (0, 0)),
            pl.BlockSpec((block, width), lambda i: (i, 0)),
        ],
        out_specs=pl.BlockSpec((length, cols), lambda i: (0, 0)),
        scratch_shapes=[
            pltpu.VMEM((heads, length, HEAD_DIM), jnp.float32),
            pltpu.VMEM((heads, length, HEAD_DIM), jnp.float32),
        ],
        cost_estimate=attend_cost(length, cols, 10),
        name="attend_back",
    )(prefix, whole, grads)


def after(value, *others):
    return lax.optimization_barrier((value,) + others)[0]


def flip(values, bit):
    count = lax.axis_size("dp")
    return lax.ppermute(values, "dp", [(i, i ^ bit) for i in range(count)])


def near_groups():
    count = lax.axis_size("dp")
    return [[i, i ^ 1] for i in range(count) if not i & 1]


def gather_near(shard):
    return lax.all_gather(shard, "dp", axis=0, axis_index_groups=near_groups())


def scatter_near(parts):
    shape = parts.shape[1:]
    total = lax.psum_scatter(
        parts.reshape(-1, shape[-1]),
        "dp",
        scatter_dimension=0,
        axis_index_groups=near_groups(),
        tiled=True,
    )
    return total.reshape(shape)


def both_rows(own):
    return jnp.concatenate([own, flip(own, 2)], 0)


def sum_pair(partial_sums):
    size = partial_sums.shape[0] // 2
    received = flip(partial_sums, 2)
    return partial_sums.astype(jnp.float32) + jnp.concatenate(
        [received[size:], received[:size]], 0
    ).astype(jnp.float32)


def sum_own(partial_sums):
    size = partial_sums.shape[0] // 2
    received = flip(partial_sums[size:], 2)
    return partial_sums[:size].astype(jnp.float32) + received.astype(jnp.float32)


def shards(
    tokens,
    cotangent,
    routes,
    prefix,
    qkv_weight,
    mix_weight,
    up_weight,
    down_weight,
    dense_gain,
    expert_up,
    expert_down,
    expert_gain,
    centroids,
):
    f32, low = jnp.float32, jnp.bfloat16
    micro_count, _, rows_dev, width = tokens.shape
    dp_count = lax.axis_size("dp")
    experts = lax.axis_size("expert")
    capacity = max(2, 5 * rows_dev // (4 * experts))
    length = rows_dev * dp_count
    mine = width // dp_count
    block = min(256, length)
    micros = range(micro_count)
    slot_ids = jnp.arange(experts * capacity, dtype=jnp.int32)
    expert_ids = jnp.arange(experts, dtype=jnp.int32)
    up_ex, down_ex, centroid = (expert_up[0], expert_down[0], centroids[0])
    gain_ex = expert_gain[0].astype(f32)

    places, grad_rows = ([], [])
    for micro in micros:
        route = routes[micro, 0, :, 0]
        onehot = (route[:, None] == expert_ids[None, :]).astype(jnp.int32)
        rank = jnp.sum((jnp.cumsum(onehot, 0) - 1) * onehot, 1)
        slot = route * capacity + rank
        place = (slot[None, :] == slot_ids[:, None]).astype(low)
        places.append(place)
        grad_sent = jnp.dot(
            place, cotangent[micro, 0].astype(low), preferred_element_type=f32
        ).astype(low)
        grad_rows.append(both_rows(swap_experts(grad_sent)))

    order_a, order_b = bit_orders()
    rows_qkv = qkv_weight.shape[0]
    by_dest = (
        qkv_weight.reshape(rows_qkv, 3, dp_count, mine)
        .transpose(0, 2, 1, 3)
        .reshape(rows_qkv, 3 * width)
    )
    half = 3 * width // 2
    gain_cols = jnp.pad(dense_gain.T, ((0, 0), (0, 126)))
    first = turn_gather(jnp.concatenate([by_dest, gain_cols], 1))
    part_a = spread(first[:, :, :half], order_a)
    part_b = spread(first[:, :, half:], order_b)
    qkv_pieces = dict(part_b)
    full_qkv = assemble(
        [(mask, jnp.concatenate([piece, qkv_pieces[mask][:, :, :half]], 2)) for mask, piece in part_a]
    )
    mix_dp = turn_gather(mix_weight)
    full_qkv = after(full_qkv, mix_dp)
    full_gain = assemble([(mask, piece[:, :, half:]) for mask, piece in part_b])
    gains = full_gain[:, :2].T.astype(f32)
    full_mix = assemble(spread(mix_dp, order_a))
    up_pieces = spread(gather_dp(up_weight), order_a)
    down_pieces = spread(gather_dp(down_weight), order_b)
    full_up, full_down = (assemble(up_pieces), assemble(down_pieces))
    hops = [
        [piece for pieces in (up_pieces, down_pieces) for _, piece in pieces[start : 2 * start]]
        for start in (1, 2)
    ]

    up_both, down_both = ([], [])
    for layer in range(2):
        up_near = gather_near(after(up_ex[layer], first))
        up_both.append(jnp.concatenate([up_near[0], up_near[1]], 1))
        down_both.append(gather_near(after(down_ex[layer], first)).reshape(-1, width))

    dense = []
    slots_in = []
    sends, mixes = ([], [])
    for micro in micros:
        source = tokens[micro, 0]
        if micro > 0:
            source = after(source, slots_in[micro - 1])
        inputs = source.astype(f32)
        normed = layer_norm(inputs, gains[0]).astype(low)
        qkv = jnp.dot(normed, full_qkv, preferred_element_type=f32).astype(low)
        blocks = qkv.reshape(rows_dev, dp_count, 3 * mine).transpose(1, 0, 2)
        whole = swap_heads(blocks).reshape(length, 3 * mine)
        if micro == 0:
            whole = after(whole, *hops[0])
        mixed = attend(whole, prefix[micro], block).reshape(dp_count, rows_dev, mine)
        mixed = swap_heads(mixed)
        mixes.append(mixed)
        if micro == 0:
            mixed = after(mixed, *hops[1])
        mixed = mixed.transpose(1, 0, 2).reshape(rows_dev, width)
        attn = jnp.dot(mixed, full_mix, preferred_element_type=f32)
        resid = inputs + attn
        normed2 = layer_norm(resid, gains[1]).astype(low)
        pre = jnp.dot(normed2, full_up, preferred_element_type=f32)
        hidden = gelu(pre).astype(low)
        ffn = jnp.dot(hidden, full_down, preferred_element_type=f32)
        dense_out = resid + ffn
        sent = jnp.dot(places[micro], dense_out.astype(low), preferred_element_type=f32).astype(low)
        dense.append((inputs, normed, whole, mixed, attn, resid, ffn, normed2, pre, hidden, dense_out))
        sends.append(sent)
        slots_in.append(swap_experts(sent))

    slot_count = experts * capacity
    first_stage = []
    for micro in micros:
        rows = both_rows(slots_in[micro])
        if micro > 0:
            rows = after(rows, first_stage[micro - 1][-1])
        sig = jax.nn.sigmoid(jnp.dot(rows, centroid, preferred_element_type=f32))[:, None]
        state0 = rows.astype(f32)
        z0 = layer_norm(state0, gain_ex[0]).astype(low)
        pre0 = jnp.dot(z0, up_both[0], preferred_element_type=f32)
        h0 = gelu(pre0).astype(low)
        out0 = jnp.dot(h0, down_both[0], preferred_element_type=f32).astype(low)
        first_stage.append((rows, sig, z0, pre0, h0, out0))
    second_stage = []

    def run_second(micro, *others):
        rows, sig = first_stage[micro][:2]
        total = sum_pair(first_stage[micro][-1])
        total = after(total, *others)
        state1 = rows.astype(f32) + total
        z1 = layer_norm(state1, gain_ex[1]).astype(low)
        pre1 = jnp.dot(z1, up_both[1], preferred_element_type=f32)
        h1 = gelu(pre1).astype(low)
        out1 = jnp.dot(h1, down_both[1], preferred_element_type=f32).astype(low)
        incoming = grad_rows[micro].astype(f32)
        grad2 = incoming * sig
        grad_y = grad2.astype(low)
        pre_grad = gelu_back(pre1, contract_cols(grad_y, down_both[1])).astype(low)
        normed_part = contract_cols(pre_grad, up_both[1]).astype(low)
        second_stage.append((state1, out1, incoming, grad2, z1, h1, grad_y, pre_grad, normed_part))

    hidden_dev = up_ex.shape[2]
    hidden_halves = (slice(0, hidden_dev), slice(hidden_dev, 2 * hidden_dev))

    def grad_halves(lefts, rights, split_left):
        left, right = (jnp.concatenate(parts, 0) for parts in (lefts, rights))
        return [
            contract_rows(left[:, half] if split_left else left, right if split_left else right[:, half])
            for half in hidden_halves
        ]

    def join_halves(down_parts, up_parts):
        return jnp.stack([jnp.stack(parts) for parts in zip(down_parts, up_parts)]).astype(low)

    gain_ones = []
    third_stage = []

    def run_third(micro, *others):
        rows, sig, z0, pre0, h0, _ = first_stage[micro]
        state1, out1, incoming, grad2 = second_stage[micro][:4]
        total = sum_pair(second_stage[micro][-1])
        total = after(total, *others)
        state_grad, gain_grad = norm_back(state1, gain_ex[1], total)
        grad1 = grad2 + state_grad
        grad_y = grad1.astype(low)
        pre_grad = gelu_back(pre0, contract_cols(grad_y, down_both[0])).astype(low)
        normed_part = contract_cols(pre_grad, up_both[0]).astype(low)
        third_stage.append((grad1, grad_y, pre_grad, normed_part))
        gain_ones.append(gain_grad)
    own_grads = []
    branches = []

    def run_own(micro, *others):
        rows, sig = first_stage[micro][:2]
        state1, out1, incoming = second_stage[micro][:3]
        grad1, normed_part = (third_stage[micro][i] for i in (0, 3))
        normed_grad = after(sum_own(normed_part), *others)
        own_rows = rows[:slot_count].astype(f32)
        state_grad, gain_grad = norm_back(own_rows, gain_ex[0], normed_grad)
        own_sig = sig[:slot_count]
        state2 = state1[:slot_count] + sum_own(out1)
        branches.append((own_sig * state2).astype(low))
        score_grad = jnp.sum(incoming[:slot_count] * state2, 1, keepdims=True)
        score_grad = score_grad * own_sig * (1.0 - own_sig)
        row_grad = grad1[:slot_count] + state_grad + score_grad * centroid.astype(f32)
        cent_grad = jnp.sum(score_grad * own_rows, 0)
        own_grads.append((row_grad.astype(low), gain_grad, cent_grad))

    gain_sums, resid_grads, late = ([], [], [])
    input_grads = []
    kept = []
    kept_dense = []
    order_c, order_d = (order_a[::-1], order_b[::-1])
    whole_grads = []

    def run_ffn_back(micro):
        inputs, normed, whole, mixed, attn, resid, ffn, normed2, pre, hidden, _ = dense[micro]
        grad_back = swap_experts(own_grads[micro][0])
        after_grad = cotangent[micro, 0] + contract_rows(places[micro], grad_back)
        ffn_low = after_grad.astype(low)
        if micro == micro_count - 1:
            ffn_low, layer_sums[1] = lax.optimization_barrier((ffn_low, layer_sums[1]))
            ffn_low = after(ffn_low, *(terms[1] for terms in kept))
        hidden_grad = contract_cols(ffn_low, full_down)
        pre_grad = gelu_back(pre, hidden_grad).astype(low)
        normed2_grad = contract_cols(pre_grad, full_up)
        resid_part, gain2_grad = norm_back(resid, gains[1], normed2_grad)
        resid_grad = after_grad + resid_part
        attn_low = resid_grad.astype(low)
        kept_dense.append((normed2, pre_grad, hidden, ffn_low))
        resid_grads.append((resid_grad, attn_low, gain2_grad))

    def run_attend_back(micro):
        inputs, normed, whole, mixed = dense[micro][:4]
        resid_grad, attn_low, gain2_grad = resid_grads[micro]
        mixed_grad = contract_cols(attn_low, full_mix).astype(low)
        mixed_grad = mixed_grad.reshape(rows_dev, dp_count, mine).transpose(1, 0, 2)
        mixed_grad = swap_heads(mixed_grad).reshape(length, mine)
        if micro == micro_count - 1:
            joined = [jnp.concatenate(parts, 0) for parts in zip(*kept_dense)]
            down_start = scatter_start(contract_rows(joined[2], joined[3]).astype(low), order_c)
            up_low = contract_rows(joined[0], joined[1]).astype(low)
            mixed_grad = after(mixed_grad, down_start[0], up_low)
            late.extend((down_start, up_low))
        whole_grad = attend_back(whole, mixed_grad, prefix[micro], block)
        whole_grads.append(whole_grad)
        qkv_grad = swap_heads(whole_grad.reshape(dp_count, rows_dev, 3 * mine))
        qkv_grad = qkv_grad.transpose(1, 0, 2).reshape(rows_dev, 3 * width)
        if micro == micro_count - 1:
            qkv_grad, layer_sums[0] = lax.optimization_barrier((qkv_grad, layer_sums[0]))
        normed_grad = contract_cols(qkv_grad, full_qkv)
        input_part, gain1_grad = norm_back(inputs, gains[0], normed_grad)
        input_grads.append(resid_grad + input_part)
        gain_sums.append(jnp.stack([gain1_grad, gain2_grad]))
        kept.append((normed, qkv_grad, mixed, attn_low))

    last = micro_count - 1
    for micro in micros:
        if micro < last:
            run_second(micro, mixes[micro + 1])
            run_third(micro, sends[micro + 1])
            run_own(micro)
            run_ffn_back(micro)
        else:
            run_second(micro, *(resid_grads[-1][1:2] if micro else ()))
    for micro in micros[:-1]:
        run_attend_back(micro)
    layer_grads, layer_sums = ([None, None], [None, None])
    by_stage = list(zip(*second_stage))
    layer_grads[1] = join_halves(
        grad_halves(by_stage[5], by_stage[6], True), grad_halves(by_stage[4], by_stage[7], False)
    )
    run_third(last, layer_grads[1])
    by_first, by_third = (list(zip(*first_stage)), list(zip(*third_stage)))
    layer_grads[0] = join_halves(
        grad_halves(by_first[4], by_third[1], True), grad_halves(by_first[2], by_third[2], False)
    )
    for layer in (1, 0):
        layer_sums[layer] = scatter_near(layer_grads[layer])
    run_own(last, *whole_grads)
    run_ffn_back(last)
    run_attend_back(last)
    down_start, up_low = late
    down_sum, up_sum = ([total[i].astype(f32) for total in layer_sums] for i in range(2))
    gain_acc, gain_one = (sum(gain_sums), sum(gain_ones))
    joined = [jnp.concatenate(parts, 0) for parts in zip(*kept)]
    down_out = scatter_end(down_start)
    up_out = scatter_rows(up_low, order_d)
    mix_low = contract_rows(joined[2], joined[3]).astype(low)
    qkv_low = contract_rows(joined[0], joined[1]).astype(low)
    qkv_mix = scatter_dp(
        jnp.concatenate(
            [
                scatter_middle(scatter_start(part, order))
                for part, order in (
                    (qkv_low[:, :half], order_c),
                    (qkv_low[:, half:], order_d),
                    (mix_low, order_d),
                )
            ],
            1,
        )
    )
    mix_out = qkv_mix[:, 3 * width :]
    qkv_out = (
        qkv_mix[:, : 3 * width].reshape(rows_qkv, dp_count, 3, mine)
        .transpose(0, 2, 1, 3)
        .reshape(rows_qkv, 3 * width)
    )

    output_list = []
    stat_list = []
    for micro in micros:
        attn, ffn, dense_out = (dense[micro][i] for i in (4, 6, 10))
        returned = swap_experts(branches[micro])
        branch = contract_rows(places[micro], returned)
        final = dense_out + branch
        output_list.append(final.astype(low))
        stat_list.append(jnp.stack([jnp.sum(v * v) for v in (final, attn, ffn, branch)]))

    small = jnp.concatenate(
        [
            jnp.stack(stat_list, 1).reshape(-1),
            sum(part[1] for part in own_grads),
            sum(part[2] for part in own_grads),
            0.5 * gain_one,
        ]
    )
    small = sum_small(small)
    stats = 4 * micro_count
    branch_rms = jnp.sqrt(small[:stats] / (length * width)).reshape(4, micro_count, 1)
    ex_gain = jnp.stack([small[stats : stats + width], small[stats + 2 * width :]])
    gain_sum = sum_small(gain_acc)
    for bit in order_a:
        gain_sum = gain_sum + swap(gain_sum, bit)
    device = lax.axis_index("dp") * experts + lax.axis_index("expert")
    gain_out = lax.dynamic_index_in_dim(
        gain_sum.reshape(2, dp_count * experts, -1), device, 1, keepdims=False
    )
    return (
        jnp.stack(output_list)[:, None],
        jnp.stack(input_grads)[:, None],
        qkv_out,
        mix_out,
        up_out,
        down_out,
        gain_out,
        jnp.stack(up_sum)[None],
        jnp.stack(down_sum)[None],
        ex_gain[None],
        small[None, stats + width : stats + 2 * width],
        branch_rms,
    )


def solution(mesh):
    return jax.shard_map(
        shards,
        mesh=mesh,
        in_specs=(
            P(None, "expert", "dp", None),
            P(None, "expert", "dp", None),
            P(None, "expert", "dp", None),
            P(None, "expert"),
            P(("dp", "expert"), None),
            P(("dp", "expert"), None),
            P(("dp", "expert"), None),
            P(("dp", "expert"), None),
            P(None, ("dp", "expert")),
            P("expert", None, None, "dp"),
            P("expert", None, "dp", None),
            P("expert", None, None),
            P("expert", None),
        ),
        out_specs=(
            P(None, "expert", "dp", None),
            P(None, "expert", "dp", None),
            P(("dp", "expert"), None),
            P(("dp", "expert"), None),
            P(("dp", "expert"), None),
            P(("dp", "expert"), None),
            P(None, ("dp", "expert")),
            P("expert", None, None, "dp"),
            P("expert", None, "dp", None),
            P("expert", None, None),
            P("expert", None),
            P(None, None, "expert"),
        ),
        check_vma=False,
    )
```
